256 devices in a mesh: group: 8 (over x, core), expert: 32 (over z, y).
Axes of the slice: x: 4, y: 4, z: 8, core: 2. Of those that a mesh axis runs over, the one named last changes fastest.
Arguments:
- out_grad: bfloat16 [65536, 3584], P(('group', 'expert')), may hold values from -6 to 6
- gates: float32 [65536, 8], P(('group', 'expert')), may hold values from 0.05 to 0.6
- routes: int32 [65536, 8], P(('group', 'expert')), may hold values from 0 to 95, all different within a row
- copy_pick: int32 [65536, 8], P(('group', 'expert')), may hold values from 0 to 839
- replica_plan: int32 [32], replicated, may hold values from 0 to 23, as said below
- down_weight: bfloat16 [32, 1024, 3584], P('expert'), as said below
- saved_hidden: bfloat16 [8, 32, 32, 20, 1024], P('group', 'expert'), may hold values from -0.75 to 0.75
Outputs:
- route_grad: float32 [65536, 8], P(('group', 'expert'))
- hidden_grad: bfloat16 [8, 32, 32, 20, 1024], P('group', 'expert')
- copy_grad: bfloat16 [32, 1024, 3584], P('expert', 'group')
The draws below stay inside these ranges and needn't reach their ends.
Inputs may be any that keep to these rules, and one draw needn't show every extreme that they name: `replica_plan`: every expert 0 to 23 is served by at least one slot; exactly 2 experts are served by more than one slot. `down_weight`: slots that serve the same expert hold equal weights.
All inputs are finite; a program needn't handle non-finite values.
Results may differ from the reference program's by a relative error of at most 0.019.
Values may be sent and summed in bfloat16 or wider, within the bound.
A program may use at most 128 MiB of HBM per device.

```python
import jax
import jax.numpy as jnp
from jax import lax

D = 3584
F = 1024
K = 8
HOT = 2
TOK_DEV = 256
GROUPS = 8
SLOTS = 32
EXPERTS = 24
ALL_EXPERTS = 96
TOKENS = 65536
CAP = 20


def plan_table(key):
    extra_slots = SLOTS - EXPERTS
    key_hot, key_more, key_order = jax.random.split(jax.random.fold_in(key, 11), 3)
    hot_experts = jax.random.permutation(key_hot, EXPERTS)[:HOT].astype(jnp.int32)
    more_copies = jax.random.randint(key_more, (extra_slots - HOT,), 0, HOT)
    extras = jnp.concatenate([hot_experts, hot_experts[more_copies]])
    all_slots = jnp.concatenate([jnp.arange(EXPERTS, dtype=jnp.int32), extras])
    return jax.random.permutation(key_order, all_slots).astype(jnp.int32)


def draw_replica_plan(key, part):
    return plan_table(key)


def draw_down_weight(key, part):
    slot_plan = plan_table(key)
    weight_key = jax.random.fold_in(key, 23)
    logical = jnp.clip(jax.random.normal(weight_key, (EXPERTS, F, D), jnp.float32), -4.0, 4.0)
    logical = logical * D ** (-0.5)
    return logical[slot_plan].astype(jnp.bfloat16)


def with_ends(drawn, stream_key, least, high):
    longest = drawn.shape.index(max(drawn.shape))
    spots = []
    for shift in (0, 1):
        where = [jax.random.randint(jax.random.fold_in(stream_key, axis), (), 0, length) for axis, length in enumerate(drawn.shape)]
        where[longest] = (where[longest] + shift) % drawn.shape[longest]
        spots.append(tuple(where))
    return drawn.at[spots[0]].set(least).at[spots[1]].set(high)


def steps_of(rng, shape, cuts, least, largest):
    def one(axis_at, parts):
        draws = jax.random.uniform(jax.random.fold_in(jax.random.fold_in(rng, 6), axis_at), (parts,), jnp.float32, least / len(cuts), largest / len(cuts))
        return jnp.repeat(jnp.exp(draws), shape[axis_at] // parts).reshape((-1,) + (1,) * (len(shape) - axis_at - 1))

    gain = one(*cuts[0])
    for cut in cuts[1:]:
        gain = gain * one(*cut)
    return gain


def picks_of(stream_key, rows, count, top, lift):
    sequence = jax.random.permutation(jax.random.fold_in(stream_key, 1), count)
    favour = sequence
    for power in range(3):
        favour = favour * favour // count
    favour = favour * lift // count
    chance = jax.random.randint(jax.random.fold_in(stream_key, 2), (rows, count), 0, 4096) + favour
    holders = jax.random.permutation(jax.random.fold_in(stream_key, 3), rows)[jnp.arange(count) % rows]
    chance = jnp.where(jnp.arange(rows)[:, None] == holders[None, :], 1 << 14, chance)
    priority = chance * count + jnp.arange(count)
    return lax.top_k(priority.astype(jnp.int32), top)[1].astype(jnp.int32)


def normal_values(own_key, dims, deviation, most, shards=(), held_as=jnp.bfloat16):
    drawn = jax.random.normal(own_key, dims, jnp.float32) * deviation
    if len(shards) > 0:
        drawn = steps_of(own_key, dims, shards, -0.22, 0.18) * drawn
    return jnp.clip(drawn, min=-most, max=most).astype(held_as)


def setup_inputs(seed: int = 0) -> dict:
    seeds = jax.random.split(jax.random.key(seed), 8)
    out_grad = normal_values(seeds[0], (TOKENS, D), 1.0, 6.0, ((0, 256),))
    gates = jnp.clip(0.05 + 0.55 * jax.random.uniform(seeds[1], (TOKENS, K), jnp.float32) ** steps_of(seeds[1], (TOKENS, K), ((0, 256),), -0.2, 0.2), 0.05, 0.6)
    routes = picks_of(seeds[2], TOKENS, ALL_EXPERTS, K, 1365)
    copy_pick = with_ends(jax.random.randint(seeds[3], (TOKENS, K), 0, 840), jax.random.fold_in(seeds[3], 1), 0, 839).astype(jnp.int32)
    replica_plan = draw_replica_plan(jax.random.fold_in(seeds[7], 71), 0)
    down_weight = draw_down_weight(jax.random.fold_in(seeds[7], 71), 0)
    saved_hidden = normal_values(seeds[6], (GROUPS, SLOTS, SLOTS, CAP, F), 0.125, 0.75, ((0, 8), (1, 32)))
    return {"out_grad": out_grad, "gates": gates, "routes": routes, "copy_pick": copy_pick, "replica_plan": replica_plan, "down_weight": down_weight, "saved_hidden": saved_hidden}


def slot_layout(replica_plan):
    slot_count = replica_plan.shape[0]
    slot_ids = jnp.arange(slot_count, dtype=jnp.int32)
    same_expert = replica_plan[:, None] == replica_plan[None, :]
    earlier_slot = slot_ids[None, :] < slot_ids[:, None]
    ordinal = jnp.sum(same_expert & earlier_slot, axis=1).astype(jnp.int32)
    return slot_ids, same_expert, ordinal


def route_slots(routes, copy_pick, replica_plan, expert_count):
    slot_ids, same_expert, ordinal = slot_layout(replica_plan)
    serves = replica_plan == routes[..., None]
    copies = jnp.sum(serves, axis=-1).astype(jnp.int32)
    inside = routes < expert_count
    chosen = copy_pick % jnp.maximum(copies, 1)
    slot_match = serves & (ordinal == chosen[..., None]) & inside[..., None]
    slot_of = jnp.sum(jnp.where(slot_match, slot_ids, 0), axis=-1).astype(jnp.int32)
    return slot_match, slot_of, inside


def route_ranks(slot_match):
    onehot = slot_match.astype(jnp.int32)
    earlier = jnp.cumsum(onehot, axis=-2) - onehot
    return jnp.sum(earlier * onehot, axis=-1).astype(jnp.int32)


def reference(out_grad, gates, routes, copy_pick, replica_plan, down_weight, saved_hidden):
    slot_count = SLOTS
    per_group = slot_count * TOK_DEV * K
    held_count = slot_count * slot_count * CAP
    slot_match, slot_of, inside = route_slots(routes, copy_pick, replica_plan, EXPERTS)
    match_dev = slot_match.reshape(GROUPS * slot_count, TOK_DEV * K, slot_count)
    route_rank = route_ranks(match_dev).reshape(GROUPS, per_group)
    slot_group = slot_of.reshape(GROUPS, per_group)
    kept_route = inside.reshape(GROUPS, per_group) & (route_rank < CAP)
    route_ids = jnp.arange(per_group, dtype=jnp.int32)
    source_dev = route_ids // (TOK_DEV * K)
    position = (slot_group * slot_count + source_dev[None, :]) * CAP + route_rank
    position = jnp.where(kept_route, position, held_count).astype(jnp.int32)
    grad_groups = out_grad.reshape(GROUPS, slot_count * TOK_DEV, D)
    gate_groups = gates.reshape(GROUPS, per_group)
    hidden_groups = saved_hidden.reshape(GROUPS, slot_count, slot_count * CAP, F)
    _, same_expert, _ = slot_layout(replica_plan)

    def one_group(grad_total, group_items):
        grad_rows, gate_rows, place, kept, held_hidden = group_items
        source_route = jnp.full((held_count,), per_group, jnp.int32).at[place].set(route_ids, mode="drop")
        occupied = source_route < per_group
        safe_route = jnp.where(occupied, source_route, 0)
        grad_held = jnp.where(occupied[:, None], grad_rows[safe_route // K], 0).astype(jnp.bfloat16)
        gate_held = jnp.where(occupied, gate_rows[safe_route], 0.0).astype(jnp.bfloat16)
        grad_held = grad_held.reshape(slot_count, slot_count * CAP, D)
        gate_held = gate_held.reshape(slot_count, slot_count * CAP)

        def one_slot(inputs):
            slot_rows, slot_gate, slot_hidden, weight_mat = inputs
            projected = lax.dot_general(slot_rows, weight_mat, (((1,), (1,)), ((), ())), preferred_element_type=jnp.float32)
            gate_f = slot_gate.astype(jnp.float32)[:, None]
            slot_grad = (gate_f * projected).astype(jnp.bfloat16)
            route_score = jnp.sum(projected * slot_hidden.astype(jnp.float32), axis=1)
            scaled = (gate_f * slot_rows.astype(jnp.float32)).astype(jnp.bfloat16)
            partial_sum = lax.dot_general(slot_hidden, scaled, (((0,), (0,)), ((), ())), preferred_element_type=jnp.float32)
            return slot_grad, route_score, partial_sum.astype(jnp.bfloat16)

        slot_grad, route_score, partial_sum = lax.map(one_slot, (grad_held, gate_held, held_hidden, down_weight))
        score_flat = jnp.concatenate([route_score.reshape(-1), jnp.zeros((1,), jnp.float32)])
        group_grad = jnp.where(kept, score_flat[place], 0.0)
        grad_total = grad_total + lax.optimization_barrier(partial_sum).astype(jnp.float32)
        return grad_total, (slot_grad, group_grad)

    start_total = jnp.zeros((slot_count, F, D), jnp.float32)
    grad_total, outputs = lax.scan(one_group, start_total, (grad_groups, gate_groups, position, kept_route, hidden_groups))
    slot_grads, group_grads = outputs
    group_sum = lax.optimization_barrier(grad_total.astype(jnp.bfloat16)).astype(jnp.float32)
    copy_grad = jnp.einsum("st,tfd->sfd", same_expert.astype(jnp.float32), group_sum, precision=lax.Precision.HIGHEST).astype(jnp.bfloat16)
    route_grad = group_grads.reshape(TOKENS, K)
    hidden_grad = slot_grads.reshape(GROUPS, slot_count, slot_count, CAP, F)
    return route_grad, hidden_grad, copy_grad
```

```python
import functools

import jax
import jax.numpy as jnp
from jax import lax
from jax.experimental import pallas as pl
from jax.experimental.pallas import tpu as pltpu
from jax.sharding import PartitionSpec as P

CORES = 2
YS = 4
LANES = 128
HEAD = 16
CHUNK = 512
COLS = CHUNK + LANES
MESH = pl.DeviceIdType.MESH
F32 = jnp.float32
BF16 = jnp.bfloat16


def iota(shape, dim):
    return lax.broadcasted_iota(jnp.int32, shape, dim)


def mm(a, b):
    return lax.dot_general(a, b, (((1,), (0,)), ((), ())), preferred_element_type=F32)


def mm_nt(a, b):
    return lax.dot_general(a, b, (((1,), (1,)), ((), ())), preferred_element_type=F32)


def onehot(mask):
    return jnp.where(mask, 1.0, 0.0).astype(BF16)


def kernel(
    dims,
    og_hbm,
    w_hbm,
    h_hbm,
    gates_ref,
    routes_ref,
    pick_ref,
    plan_ref,
    rg_ref,
    hg_ref,
    cg_ref,
    og_v,
    w_v,
    h_v,
    hq,
    ht,
    s_head,
    s_tail,
    shuffle,
    sbuf,
    rbuf,
    gate_out,
    gate_in,
    score_out,
    score_in,
    rows_b,
    scaled_b,
    gcol,
    proj,
    hg_v,
    pb,
    pr,
    xb,
    xr,
    gsum,
    yr,
    tb,
    zr,
    ub,
    vb,
    wb,
    ya,
    ld_sem,
    own_sem,
    row_s,
    row_r,
    gate_s,
    gate_r,
    pair_s,
    pair_r,
    x_s,
    x_r,
    y_s,
    y_r,
    z_s,
    z_r,
    v_s,
    v_r,
    w_s,
    w_r,
    score_s,
    score_r,
):
    groups, slots, cap, toks, topk, width, hidden = dims
    xs, zs = groups // CORES, slots // YS
    tail = cap - HEAD
    chunks = width // CHUNK
    n_head, n_tail = slots * HEAD, slots * tail
    n_rows = n_head + n_tail
    piece = hidden // groups
    zrows = piece // zs
    ycols = CHUNK // YS

    g = lax.axis_index("group")
    e = lax.axis_index("expert")
    x, core = g // CORES, g % CORES
    z, y = e // YS, e % YS
    mate = (x * CORES + (1 - core), e)

    def plane(k):
        return (g, lax.rem(z + k // YS, zs) * YS + lax.rem(y + k % YS, YS))

    def plane_slot(k):
        return lax.rem(z + k // YS, zs) * YS + lax.rem(y + k % YS, YS)

    def xdev(k):
        return (lax.rem(x + k, xs) * CORES + core, e)

    def ydev(k):
        return (g, z * YS + lax.rem(y + k, YS))

    def zdev(k):
        return (g, lax.rem(z + k, zs) * YS + y)

    def remote(src, dst, ssem, rsem, dev):
        pltpu.make_async_remote_copy(
            src_ref=src, dst_ref=dst, send_sem=ssem, recv_sem=rsem, device_id=dev, device_id_type=MESH
        ).start()

    def await_bytes(ref, sem):
        pltpu.make_async_copy(ref, ref, sem).wait()

    ld_og = pltpu.make_async_copy(og_hbm, og_v, ld_sem.at[0])
    ld_h = pltpu.make_async_copy(h_hbm, h_v, ld_sem.at[1])
    ld_w = pltpu.make_async_copy(w_hbm, w_v, ld_sem.at[2])
    ld_og.start()
    ld_h.start()
    ld_w.start()

    barrier = pltpu.get_barrier_semaphore()

    def greet(k, carry):
        pl.semaphore_signal(barrier, inc=1, device_id=plane(k), device_id_type=MESH)
        return carry

    lax.fori_loop(1, slots, greet, 0)
    pl.semaphore_signal(barrier, inc=1, device_id=mate, device_id_type=MESH)
    for k in range(1, xs):
        pl.semaphore_signal(barrier, inc=1, device_id=xdev(k), device_id_type=MESH)

    plan_row = plan_ref[...].astype(F32)
    si, ti = iota((slots, slots), 0), iota((slots, slots), 1)
    plan_col = jnp.sum(jnp.where(si == ti, plan_row, 0.0), axis=1, keepdims=True)
    same = jnp.where(plan_col == plan_row, 1.0, 0.0)
    reps_col = jnp.sum(same, axis=1, keepdims=True)
    reps_row = jnp.sum(same, axis=0, keepdims=True)
    ord_col = jnp.sum(jnp.where(ti < si, same, 0.0), axis=1, keepdims=True)
    ord_row = jnp.sum(jnp.where(si < ti, same, 0.0), axis=0, keepdims=True)
    first_row = jnp.where((reps_row > 1.0) & (ord_row == 0.0), 1.0, 0.0)
    hot_rank = jnp.sum(jnp.where(plan_row < plan_col, first_row, 0.0), axis=1, keepdims=True)
    slot_id = iota((slots, 1), 0)

    def at_slot(col, slot):
        return jnp.sum(jnp.where(slot_id == slot, col, 0.0), axis=0, keepdims=True)

    in_table = [jnp.where((reps_col > 1.0) & (hot_rank == float(h)), 1.0, 0.0) for h in range(2)]
    y_weight = [[at_slot(in_table[h], z * YS + yy) for h in range(2)] for yy in range(YS)]
    my_hot = at_slot(in_table[0] + in_table[1], e) > 0.0

    inv_reps = 1.0 / reps_col

    def match(k):
        route = routes_ref[k : k + 1, :].astype(F32)
        pick = pick_ref[k : k + 1, :].astype(F32)
        chosen = pick - jnp.floor((pick + 0.5) * inv_reps) * reps_col
        return (plan_col == route) & (chosen == ord_col)

    taken = jnp.zeros((slots, toks), F32)
    gate_of = jnp.zeros((slots, toks), F32)
    for k in range(topk):
        hit = match(k)
        taken = jnp.where(hit, 1.0, taken)
        gate_of = jnp.where(hit, gates_ref[k : k + 1, :], gate_of)
    before = onehot(iota((toks, toks), 0) < iota((toks, toks), 1))
    rank = mm(taken.astype(BF16), before)
    rank = jnp.where((taken > 0.0) & (rank < float(cap)), rank, 64.0)
    rank_b, gate_b = rank.astype(BF16), gate_of.astype(BF16)
    grow = jnp.zeros((slots, LANES), F32)
    for per, base, s_ref in ((HEAD, 0, s_head), (tail, HEAD, s_tail)):
        n = slots * per
        spread = onehot(iota((n, slots), 0) // per == iota((n, slots), 1))
        collect = onehot(iota((slots, n), 1) // per == iota((slots, n), 0))
        c_of = iota((n, 1), 0) % per + base
        sel = jnp.where(mm(spread, rank_b) == c_of.astype(F32), 1.0, 0.0)
        s_ref[...] = sel.astype(BF16)
        held = jnp.sum(sel * mm(spread, gate_b), axis=1, keepdims=True)
        grow = grow + mm(collect, jnp.where(iota((n, LANES), 1) == c_of, held, 0.0).astype(BF16))
    for s in range(slots):
        gate_out[s] = grow[s : s + 1, :]

    blocks = CHUNK // LANES
    rr, cc = iota((n_head, n_head), 0), iota((n_head, n_head), 1)
    shuffle[...] = onehot(cc == (rr // tail % blocks) * n_tail + (rr // HEAD) * tail + rr % tail)

    ld_og.wait()

    def gather(c):
        part = og_v[:, pl.ds(pl.multiple_of(c * CHUNK, CHUNK), CHUNK)]
        sbuf[c, :, :, 0:CHUNK] = mm(s_head[...], part).astype(BF16).reshape(slots, HEAD, CHUNK)
        low = mm(s_tail[...], part).astype(BF16)
        low = jnp.concatenate([low[:, i * LANES : (i + 1) * LANES] for i in range(blocks)], axis=0)
        sbuf[c, :, :, CHUNK:COLS] = mm(shuffle[...], low).astype(BF16).reshape(slots, HEAD, LANES)

    gather(0)
    pl.semaphore_wait(barrier, slots + xs - 1)

    def send_gate(k, carry):
        remote(gate_out.at[plane_slot(k)], gate_in.at[e], gate_s, gate_r, plane(k))
        return carry

    def dispatch(c, carry):
        def one(k, inner):
            remote(sbuf.at[c, plane_slot(k)], rbuf.at[c, e], row_s.at[c], row_r.at[c], plane(k))
            return inner

        lax.fori_loop(1, slots, one, 0)
        pltpu.make_async_copy(sbuf.at[c, e], rbuf.at[c, e], own_sem.at[c]).start()

        @pl.when(c + 1 < chunks)
        def _():
            gather(c + 1)

        return carry

    lax.fori_loop(1, slots, send_gate, 0)
    own_gate = pltpu.make_async_copy(gate_out.at[e], gate_in.at[e], ld_sem.at[3])
    own_gate.start()
    lax.fori_loop(0, chunks, dispatch, 0)

    ld_h.wait()
    fb = min(256, hidden)

    def order(per, back):
        n = slots * per
        r, c = iota((n, n), 0), iota((n, n), 1)
        if back:
            return onehot(c == (r % slots) * per + r // slots)
        return onehot(c == (r % per) * slots + r // per)

    fwd_head, fwd_tail = order(HEAD, False), order(tail, False)

    def reorder(f, carry):
        cols = pl.ds(pl.multiple_of(f * fb, fb), fb)
        hq[0:n_head, cols] = mm(fwd_head, h_v[0:n_head, cols]).astype(BF16)
        hq[n_head:n_rows, cols] = mm(fwd_tail, h_v[n_head:n_rows, cols]).astype(BF16)
        ht[cols, :] = hq[:, cols].T
        return carry

    lax.fori_loop(0, hidden // fb, reorder, 0)
    proj[...] = jnp.zeros_like(proj)

    await_bytes(gate_in.at[pl.ds(0, slots - 1)], gate_r)
    own_gate.wait()
    gin = gate_in[:, 0, :].astype(BF16)
    for per, base, first in ((HEAD, 0, 0), (tail, HEAD, n_head)):
        n = slots * per
        spread = onehot(iota((n, slots), 0) // per == iota((n, slots), 1))
        c_of = iota((n, 1), 0) % per + base
        picked = jnp.where(iota((n, LANES), 1) == c_of, mm(spread, gin), 0.0)
        gcol[first : first + n, :] = jnp.sum(picked, axis=1, keepdims=True)
    ld_w.wait()
    xb_rows = CORES * piece

    def from_x(c):
        await_bytes(xr.at[c], x_r.at[c])
        total = xb[c, x].astype(F32)
        for k in range(xs - 1):
            total = total + xr[c, k].astype(F32)
        total = total.astype(BF16)
        for yy in range(YS):
            gsum[c, yy] = total[:, yy * ycols : (yy + 1) * ycols]
        for k in range(1, YS):
            remote(gsum.at[c, lax.rem(y + k, YS)], yr.at[c, k - 1], y_s.at[c], y_r.at[c], ydev(k))

    def from_y(c):
        await_bytes(yr.at[c], y_r.at[c])
        for h in range(2):
            total = jnp.zeros((piece, ycols), F32)
            for yy in range(YS):
                came = gsum[c, y].astype(F32)
                for k in range(1, YS):
                    came = jnp.where(lax.rem(y + YS - k, YS) == yy, yr[c, k - 1].astype(F32), came)
                total = total + y_weight[yy][h] * came
            tb[c, :, h] = total.astype(BF16).reshape(zs, zrows, ycols)
        for k in range(1, zs):
            remote(tb.at[c, lax.rem(z + k, zs)], zr.at[c, k - 1], z_s.at[c], z_r.at[c], zdev(k))

    def from_z(c):
        await_bytes(zr.at[c], z_r.at[c])
        total = tb[c, z].astype(F32)
        for k in range(zs - 1):
            total = total + zr[c, k].astype(F32)
        total = total.astype(BF16)
        ub[c] = total
        vb[c, z] = total
        for k in range(1, zs):
            remote(ub.at[c], vb.at[c, z], v_s.at[c], v_r.at[c], zdev(k))

    def from_v(c):
        await_bytes(vb.at[c, pl.ds(0, zs - 1)], v_r.at[c])
        tables = [vb[c, :, h].reshape(piece, ycols).astype(F32) for h in range(2)]
        for yy in range(YS):
            wb[c, yy] = (y_weight[yy][0] * tables[0] + y_weight[yy][1] * tables[1]).astype(BF16)
        ya[c, y] = wb[c, y]
        for k in range(1, YS):
            remote(wb.at[c, lax.rem(y + k, YS)], ya.at[c, y], w_s.at[c], w_r.at[c], ydev(k))

    def from_w(c):
        await_bytes(ya.at[c, pl.ds(0, YS - 1)], w_r.at[c])
        for yy in range(YS):
            cols = pl.ds(pl.multiple_of(c * CHUNK + yy * ycols, ycols), ycols)
            cg_ref[:, cols] = jnp.where(my_hot, ya[c, yy].astype(F32), gsum[c, yy].astype(F32)).astype(BF16)

    def main(c, carry):
        await_bytes(rbuf.at[c, pl.ds(0, slots - 1)], row_r.at[c])
        pltpu.make_async_copy(sbuf.at[c, e], rbuf.at[c, e], own_sem.at[c]).wait()
        rows_b[0:n_head, :] = rbuf[c, :, :, 0:CHUNK].reshape(n_head, CHUNK)
        low = lax.dot_general(
            shuffle[...],
            rbuf[c, :, :, CHUNK:COLS].reshape(n_head, LANES),
            (((0,), (0,)), ((), ())),
            preferred_element_type=F32,
        ).astype(BF16)
        for i in range(blocks):
            rows_b[n_head:n_rows, i * LANES : (i + 1) * LANES] = low[i * n_tail : (i + 1) * n_tail, :]
        scaled_b[...] = (gcol[...] * rows_b[...].astype(F32)).astype(BF16)

        def partial(xx, inner):
            rows = pl.ds(pl.multiple_of(xx * xb_rows, xb_rows), xb_rows)
            out = mm(ht[rows, :], scaled_b[...]).astype(BF16)
            for cc in range(CORES):
                pb[c, cc, xx] = out[cc * piece : (cc + 1) * piece, :]
            return inner

        lax.fori_loop(0, xs, partial, 0)
        remote(pb.at[c, 1 - core], pr.at[c], pair_s.at[c], pair_r.at[c], mate)

        def accumulate(f, inner):
            rows = pl.ds(pl.multiple_of(f * fb, fb), fb)
            wcols = pl.ds(pl.multiple_of(c * CHUNK, CHUNK), CHUNK)
            proj[:, rows] += mm_nt(rows_b[...], w_v[rows, wcols])
            return inner

        lax.fori_loop(0, hidden // fb, accumulate, 0)

        await_bytes(pr.at[c], pair_r.at[c])
        for xx in range(xs):
            xb[c, xx] = (pb[c, core, xx].astype(F32) + pr[c, xx].astype(F32)).astype(BF16)
        for k in range(1, xs):
            remote(xb.at[c, lax.rem(x + k, xs)], xr.at[c, k - 1], x_s.at[c], x_r.at[c], xdev(k))

        @pl.when(c >= 1)
        def _():
            from_x(c - 1)

        return carry

    lax.fori_loop(0, chunks, main, 0)

    back_head, back_tail = order(HEAD, True), order(tail, True)

    def finish(f, score):
        cols = pl.ds(pl.multiple_of(f * fb, fb), fb)
        block = proj[:, cols]
        grad = (gcol[...] * block).astype(BF16)
        hg_v[0:n_head, cols] = mm(back_head, grad[0:n_head, :]).astype(BF16)
        hg_v[n_head:n_rows, cols] = mm(back_tail, grad[n_head:n_rows, :]).astype(BF16)
        return score + jnp.sum(block * hq[:, cols].astype(F32), axis=1, keepdims=True)

    score = lax.fori_loop(0, hidden // fb, finish, jnp.zeros((n_rows, 1), F32))
    srow = jnp.zeros((slots, LANES), F32)
    for per, base, first in ((HEAD, 0, 0), (tail, HEAD, n_head)):
        n = slots * per
        collect = jnp.where(iota((slots, n), 1) // per == iota((slots, n), 0), 1.0, 0.0)
        c_of = iota((n, 1), 0) % per + base
        put = jnp.where(iota((n, LANES), 1) == c_of, score[first : first + n, :], 0.0)
        srow = srow + lax.dot_general(
            collect, put, (((1,), (0,)), ((), ())), precision=lax.Precision.HIGHEST, preferred_element_type=F32
        )
    for s in range(slots):
        score_out[s] = srow[s : s + 1, :]

    def send_score(k, carry):
        remote(score_out.at[plane_slot(k)], score_in.at[e], score_s, score_r, plane(k))
        return carry

    lax.fori_loop(1, slots, send_score, 0)
    own_score = pltpu.make_async_copy(score_out.at[e], score_in.at[e], ld_sem.at[4])
    own_score.start()
    out_h = pltpu.make_async_copy(hg_v, hg_ref, ld_sem.at[5])
    out_h.start()

    from_x(chunks - 1)

    def each(stage):
        def run(c, carry):
            stage(c)
            return carry

        lax.fori_loop(0, chunks, run, 0)

    each(from_y)
    each(from_z)
    each(from_v)
    each(from_w)

    await_bytes(score_in.at[pl.ds(0, slots - 1)], score_r)
    own_score.wait()
    sin = score_in[:, 0, :]
    value = jnp.zeros((slots, toks), F32)
    for c in range(cap):
        value = jnp.where(rank == float(c), sin[:, c : c + 1], value)
    for k in range(topk):
        rg_ref[k : k + 1, :] = jnp.sum(jnp.where(match(k), value, 0.0), axis=0, keepdims=True)

    out_h.wait()
    await_bytes(gate_out.at[pl.ds(0, slots - 1)], gate_s)
    await_bytes(score_out.at[pl.ds(0, slots - 1)], score_s)

    def settle(c, carry):
        await_bytes(sbuf.at[c, pl.ds(0, slots - 1)], row_s.at[c])
        await_bytes(pr.at[c], pair_s.at[c])
        await_bytes(xr.at[c], x_s.at[c])
        await_bytes(yr.at[c], y_s.at[c])
        await_bytes(zr.at[c], z_s.at[c])
        await_bytes(zr.at[c], v_s.at[c])
        await_bytes(yr.at[c], w_s.at[c])
        return carry

    lax.fori_loop(0, chunks, settle, 0)


def local(groups, slots, out_grad, gates, routes, copy_pick, replica_plan, down_weight, saved_hidden):
    toks, width = out_grad.shape
    topk = routes.shape[1]
    hidden = down_weight.shape[1]
    cap = saved_hidden.shape[3]
    xs, zs = groups // CORES, slots // YS
    tail = cap - HEAD
    chunks = width // CHUNK
    n_rows = slots * cap
    n_head = slots * HEAD
    piece = hidden // groups
    zrows = piece // zs
    ycols = CHUNK // YS
    held = saved_hidden[0, 0].transpose(1, 0, 2).reshape(n_rows, hidden)
    vmem = pltpu.VMEM
    dma = pltpu.SemaphoreType.DMA
    scratch = [
        vmem((toks, width), BF16),
        vmem((hidden, width), BF16),
        vmem((n_rows, hidden), BF16),
        vmem((n_rows, hidden), BF16),
        vmem((hidden, n_rows), BF16),
        vmem((n_head, toks), BF16),
        vmem((slots * tail, toks), BF16),
        vmem((n_head, n_head), BF16),
        vmem((chunks, slots, HEAD, COLS), BF16),
        vmem((chunks, slots, HEAD, COLS), BF16),
        vmem((slots, 1, LANES), F32),
        vmem((slots, 1, LANES), F32),
        vmem((slots, 1, LANES), F32),
        vmem((slots, 1, LANES), F32),
        vmem((n_rows, CHUNK), BF16),
        vmem((n_rows, CHUNK), BF16),
        vmem((n_rows, 1), F32),
        vmem((n_rows, hidden), F32),
        vmem((n_rows, hidden), BF16),
        vmem((chunks, CORES, xs, piece, CHUNK), BF16),
        vmem((chunks, xs, piece, CHUNK), BF16),
        vmem((chunks, xs, piece, CHUNK), BF16),
        vmem((chunks, xs - 1, piece, CHUNK), BF16),
        vmem((chunks, YS, piece, ycols), BF16),
        vmem((chunks, YS - 1, piece, ycols), BF16),
        vmem((chunks, zs, 2, zrows, ycols), BF16),
        vmem((chunks, zs - 1, 2, zrows, ycols), BF16),
        vmem((chunks, 2, zrows, ycols), BF16),
        vmem((chunks, zs, 2, zrows, ycols), BF16),
        vmem((chunks, YS, piece, ycols), BF16),
        vmem((chunks, YS, piece, ycols), BF16),
        dma((6,)),
        dma((chunks,)),
        dma((chunks,)),
        dma((chunks,)),
        dma,
        dma,
        dma((chunks,)),
        dma((chunks,)),
        dma((chunks,)),
        dma((chunks,)),
        dma((chunks,)),
        dma((chunks,)),
        dma((chunks,)),
        dma((chunks,)),
        dma((chunks,)),
        dma((chunks,)),
        dma((chunks,)),
        dma((chunks,)),
        dma,
        dma,
    ]
    dims = (groups, slots, cap, toks, topk, width, hidden)
    here = pl.BlockSpec(memory_space=pltpu.VMEM)
    there = pl.BlockSpec(memory_space=pl.ANY)
    route_grad, hidden_grad, copy_grad = pl.pallas_call(
        functools.partial(kernel, dims),
        out_shape=(
            jax.ShapeDtypeStruct((topk, toks), F32),
            jax.ShapeDtypeStruct((n_rows, hidden), BF16),
            jax.ShapeDtypeStruct((piece, width), BF16),
        ),
        in_specs=[there, there, there, here, here, here, here],
        out_specs=(here, there, here),
        scratch_shapes=scratch,
        compiler_params=pltpu.CompilerParams(
            collective_id=0, has_side_effects=True, vmem_limit_bytes=63 * 2**20
        ),
        name="expert_backward",
    )(out_grad, down_weight[0], held, gates.T, routes.T, copy_pick.T, replica_plan[None, :])
    hidden_grad = hidden_grad.reshape(cap, slots, hidden).transpose(1, 0, 2)
    return route_grad.T, hidden_grad[None, None], copy_grad[None]


def solution(mesh):
    groups, slots = mesh.shape["group"], mesh.shape["expert"]
    placed = (
        P(("group", "expert"), None),
        P(("group", "expert"), None),
        P(("group", "expert"), None),
        P(("group", "expert"), None),
        P(),
        P("expert", None, None),
        P("group", "expert", None, None, None),
    )
    return jax.shard_map(
        functools.partial(local, groups, slots),
        mesh=mesh,
        in_specs=placed,
        out_specs=(
            P(("group", "expert"), None),
            P("group", "expert", None, None, None),
            P("expert", "group", None),
        ),
        check_vma=False,
    )
```

```python
import functools

import jax
import jax.numpy as jnp
from jax import lax
from jax.experimental import pallas as pl
from jax.experimental.pallas import tpu as pltpu
from jax.sharding import PartitionSpec as P

CORES = 2
YS = 4
LANES = 128
HEAD = 16
CHUNK = 512
COLS = CHUNK + LANES
MESH = pl.DeviceIdType.MESH
F32 = jnp.float32
BF16 = jnp.bfloat16


def iota(shape, dim):
    return lax.broadcasted_iota(jnp.int32, shape, dim)


def mm(a, b):
    return lax.dot_general(a, b, (((1,), (0,)), ((), ())), preferred_element_type=F32)


def mm_nt(a, b):
    return lax.dot_general(a, b, (((1,), (1,)), ((), ())), preferred_element_type=F32)


def onehot(mask):
    return jnp.where(mask, 1.0, 0.0).astype(BF16)


def kernel(
    dims,
    og_hbm,
    w_hbm,
    h_hbm,
    gates_ref,
    routes_ref,
    pick_ref,
    plan_ref,
    rg_ref,
    hg_ref,
    cg_ref,
    og_v,
    w_v,
    h_v,
    hq,
    ht,
    s_head,
    s_tail,
    shuffle,
    sbuf,
    rbuf,
    gate_out,
    gate_in,
    score_out,
    score_in,
    rows_b,
    scaled_b,
    gcol,
    proj,
    hg_v,
    pb,
    pr,
    xb,
    xr,
    gsum,
    yr,
    tb,
    zr,
    ub,
    vb,
    wb,
    ya,
    ld_sem,
    own_sem,
    row_s,
    row_r,
    gate_s,
    gate_r,
    pair_s,
    pair_r,
    x_s,
    x_r,
    y_s,
    y_r,
    z_s,
    z_r,
    v_s,
    v_r,
    w_s,
    w_r,
    score_s,
    score_r,
):
    groups, slots, cap, toks, topk, width, hidden = dims
    xs, zs = groups // CORES, slots // YS
    tail = cap - HEAD
    chunks = width // CHUNK
    n_head, n_tail = slots * HEAD, slots * tail
    n_rows = n_head + n_tail
    piece = hidden // groups
    zrows = piece // zs
    ycols = CHUNK // YS

    g = lax.axis_index("group")
    e = lax.axis_index("expert")
    x, core = g // CORES, g % CORES
    z, y = e // YS, e % YS
    mate = (x * CORES + (1 - core), e)

    def plane(k):
        return (g, lax.rem(z + k // YS, zs) * YS + lax.rem(y + k % YS, YS))

    def plane_slot(k):
        return lax.rem(z + k // YS, zs) * YS + lax.rem(y + k % YS, YS)

    def xdev(k):
        return (lax.rem(x + k, xs) * CORES + core, e)

    def ydev(k):
        return (g, z * YS + lax.rem(y + k, YS))

    def zdev(k):
        return (g, lax.rem(z + k, zs) * YS + y)

    def remote(src, dst, ssem, rsem, dev):
        pltpu.make_async_remote_copy(
            src_ref=src, dst_ref=dst, send_sem=ssem, recv_sem=rsem, device_id=dev, device_id_type=MESH
        ).start()

    def await_bytes(ref, sem):
        pltpu.make_async_copy(ref, ref, sem).wait()

    ld_og = pltpu.make_async_copy(og_hbm, og_v, ld_sem.at[0])
    ld_h = pltpu.make_async_copy(h_hbm, h_v, ld_sem.at[1])
    ld_w = pltpu.make_async_copy(w_hbm, w_v, ld_sem.at[2])
    ld_og.start()
    ld_h.start()
    ld_w.start()

    barrier = pltpu.get_barrier_semaphore()

    def greet(k, carry):
        pl.semaphore_signal(barrier, inc=1, device_id=plane(k), device_id_type=MESH)
        return carry

    lax.fori_loop(1, slots, greet, 0)
    pl.semaphore_signal(barrier, inc=1, device_id=mate, device_id_type=MESH)
    for k in range(1, xs):
        pl.semaphore_signal(barrier, inc=1, device_id=xdev(k), device_id_type=MESH)

    plan_row = plan_ref[...].astype(F32)
    si, ti = iota((slots, slots), 0), iota((slots, slots), 1)
    plan_col = jnp.sum(jnp.where(si == ti, plan_row, 0.0), axis=1, keepdims=True)
    same = jnp.where(plan_col == plan_row, 1.0, 0.0)
    reps_col = jnp.sum(same, axis=1, keepdims=True)
    reps_row = jnp.sum(same, axis=0, keepdims=True)
    ord_col = jnp.sum(jnp.where(ti < si, same, 0.0), axis=1, keepdims=True)
    ord_row = jnp.sum(jnp.where(si < ti, same, 0.0), axis=0, keepdims=True)
    first_row = jnp.where((reps_row > 1.0) & (ord_row == 0.0), 1.0, 0.0)
    hot_rank = jnp.sum(jnp.where(plan_row < plan_col, first_row, 0.0), axis=1, keepdims=True)
    slot_id = iota((slots, 1), 0)

    def at_slot(col, slot):
        return jnp.sum(jnp.where(slot_id == slot, col, 0.0), axis=0, keepdims=True)

    in_table = [jnp.where((reps_col > 1.0) & (hot_rank == float(h)), 1.0, 0.0) for h in range(2)]
    y_weight = [[at_slot(in_table[h], z * YS + yy) for h in range(2)] for yy in range(YS)]
    near_weight = [[at_slot(in_table[h], z * YS + lax.rem(y + YS - k, YS)) for h in range(2)] for k in range(YS)]
    my_hot = at_slot(in_table[0] + in_table[1], e) > 0.0

    inv_reps = 1.0 / reps_col

    def match(k):
        route = routes_ref[k : k + 1, :].astype(F32)
        pick = pick_ref[k : k + 1, :].astype(F32)
        chosen = pick - jnp.floor((pick + 0.5) * inv_reps) * reps_col
        return (plan_col == route) & (chosen == ord_col)

    taken = jnp.zeros((slots, toks), F32)
    gate_of = jnp.zeros((slots, toks), F32)
    for k in range(topk):
        hit = match(k)
        taken = jnp.where(hit, 1.0, taken)
        gate_of = jnp.where(hit, gates_ref[k : k + 1, :], gate_of)
    before = onehot(iota((toks, toks), 0) < iota((toks, toks), 1))
    rank = mm(taken.astype(BF16), before)
    rank = jnp.where((taken > 0.0) & (rank < float(cap)), rank, 64.0)
    rank_b, gate_b = rank.astype(BF16), gate_of.astype(BF16)
    parts = ((HEAD, 0, 0, s_head), (tail, HEAD, n_head, s_tail))

    def spread(per):
        n = slots * per
        return onehot(iota((n, 1), 0) // per == iota((n, slots), 1))

    def rank_of(per, base):
        return iota((slots * per, 1), 0) % per + base

    for per, base, _, s_ref in parts:
        s_ref[...] = onehot(mm(spread(per), rank_b) == rank_of(per, base).astype(F32))

    blocks = CHUNK // LANES
    rr = iota((n_head, 1), 0)
    shuffle[...] = onehot(
        iota((n_head, n_head), 1) == (rr // tail % blocks) * n_tail + (rr // HEAD) * tail + rr % tail
    )

    ld_og.wait()

    def gather(c):
        part = og_v[:, pl.ds(pl.multiple_of(c * CHUNK, CHUNK), CHUNK)]
        sbuf[c, :, :, 0:CHUNK] = mm(s_head[...], part).astype(BF16).reshape(slots, HEAD, CHUNK)
        low = mm(s_tail[...], part).astype(BF16)
        low = jnp.concatenate([low[:, i * LANES : (i + 1) * LANES] for i in range(blocks)], axis=0)
        sbuf[c, :, :, CHUNK:COLS] = mm(shuffle[...], low).astype(BF16).reshape(slots, HEAD, LANES)

    gather(0)
    pl.semaphore_wait(barrier, slots + xs - 1)

    def send_gate(k, carry):
        remote(gate_out.at[plane_slot(k)], gate_in.at[e], gate_s, gate_r, plane(k))
        return carry

    def dispatch(c, carry):
        def one(k, inner):
            remote(sbuf.at[c, plane_slot(k)], rbuf.at[c, e], row_s.at[c], row_r.at[c], plane(k))
            return inner

        lax.fori_loop(1, slots, one, 0)
        pltpu.make_async_copy(sbuf.at[c, e], rbuf.at[c, e], own_sem.at[c]).start()

        @pl.when(c + 1 < chunks)
        def _():
            gather(c + 1)

        return carry

    dispatch(0, 0)

    grow = jnp.zeros((slots, LANES), F32)
    for per, base, _, s_ref in parts:
        n = slots * per
        collect = onehot(iota((1, n), 1) // per == iota((slots, n), 0))
        held = jnp.sum(s_ref[...].astype(F32) * mm(spread(per), gate_b), axis=1, keepdims=True)
        put = jnp.where(iota((n, LANES), 1) == rank_of(per, base), held, 0.0)
        grow = grow + mm(collect, put.astype(BF16))
    for s in range(slots):
        gate_out[s] = grow[s : s + 1, :]
    lax.fori_loop(1, slots, send_gate, 0)
    own_gate = pltpu.make_async_copy(gate_out.at[e], gate_in.at[e], ld_sem.at[3])
    own_gate.start()
    lax.fori_loop(1, chunks, dispatch, 0)

    ld_h.wait()
    fb = min(256, hidden)

    def order(per, back):
        n = slots * per
        r, c = iota((n, 1), 0), iota((n, n), 1)
        if back:
            return onehot(c == (r % slots) * per + r // slots)
        return onehot(c == (r % per) * slots + r // per)

    fwd_head, fwd_tail = order(HEAD, False), order(tail, False)

    def reorder(f, carry):
        cols = pl.ds(pl.multiple_of(f * fb, fb), fb)
        hq[0:n_head, cols] = mm(fwd_head, h_v[0:n_head, cols]).astype(BF16)
        hq[n_head:n_rows, cols] = mm(fwd_tail, h_v[n_head:n_rows, cols]).astype(BF16)
        ht[cols, :] = hq[:, cols].T
        return carry

    lax.fori_loop(0, hidden // fb, reorder, 0)
    proj[...] = jnp.zeros_like(proj)

    await_bytes(gate_in.at[pl.ds(0, slots - 1)], gate_r)
    own_gate.wait()
    gin = gate_in[:, 0, :].astype(BF16)
    for per, base, first, _ in parts:
        n = slots * per
        picked = jnp.where(iota((n, LANES), 1) == rank_of(per, base), mm(spread(per), gin), 0.0)
        gcol[first : first + n, :] = jnp.sum(picked, axis=1, keepdims=True)
    ld_w.wait()
    xb_rows = CORES * piece

    def from_x(c):
        await_bytes(xr.at[c], x_r.at[c])
        total = xb[c, x].astype(F32)
        for k in range(xs - 1):
            total = total + xr[c, k].astype(F32)
        total = total.astype(BF16)
        for yy in range(YS):
            gsum[c, yy] = total[:, yy * ycols : (yy + 1) * ycols]
        for k in range(1, YS):
            remote(gsum.at[c, lax.rem(y + k, YS)], yr.at[c, k - 1], y_s.at[c], y_r.at[c], ydev(k))

    def from_y(c):
        await_bytes(yr.at[c], y_r.at[c])
        came = [gsum[c, y].astype(F32)] + [yr[c, k - 1].astype(F32) for k in range(1, YS)]
        for h in range(2):
            total = near_weight[0][h] * came[0]
            for k in range(1, YS):
                total = total + near_weight[k][h] * came[k]
            tb[c, :, h] = total.astype(BF16).reshape(zs, zrows, ycols)
        for k in range(1, zs):
            remote(tb.at[c, lax.rem(z + k, zs)], zr.at[c, k - 1], z_s.at[c], z_r.at[c], zdev(k))

    def from_z(c):
        await_bytes(zr.at[c], z_r.at[c])
        total = tb[c, z].astype(F32)
        for k in range(zs - 1):
            total = total + zr[c, k].astype(F32)
        total = total.astype(BF16)
        ub[c] = total
        vb[c, z] = total
        for k in range(1, zs):
            remote(ub.at[c], vb.at[c, z], v_s.at[c], v_r.at[c], zdev(k))

    def from_v(c):
        await_bytes(vb.at[c, pl.ds(0, zs - 1)], v_r.at[c])
        tables = [vb[c, :, h].reshape(piece, ycols).astype(F32) for h in range(2)]
        for yy in range(YS):
            wb[c, yy] = (y_weight[yy][0] * tables[0] + y_weight[yy][1] * tables[1]).astype(BF16)
        ya[c, y] = wb[c, y]
        for k in range(1, YS):
            remote(wb.at[c, lax.rem(y + k, YS)], ya.at[c, y], w_s.at[c], w_r.at[c], ydev(k))

    def from_w(c):
        await_bytes(ya.at[c, pl.ds(0, YS - 1)], w_r.at[c])
        for yy in range(YS):
            cols = pl.ds(pl.multiple_of(c * CHUNK + yy * ycols, ycols), ycols)
            cg_ref[:, cols] = jnp.where(my_hot, ya[c, yy].astype(F32), gsum[c, yy].astype(F32)).astype(BF16)

    def each(stage, start, stop):
        def run(c, carry):
            stage(c)
            return carry

        lax.fori_loop(start, stop, run, 0)

    def main(c, carry):
        await_bytes(rbuf.at[c, pl.ds(0, slots - 1)], row_r.at[c])
        pltpu.make_async_copy(sbuf.at[c, e], rbuf.at[c, e], own_sem.at[c]).wait()
        rows_b[0:n_head, :] = rbuf[c, :, :, 0:CHUNK].reshape(n_head, CHUNK)
        low = lax.dot_general(
            shuffle[...],
            rbuf[c, :, :, CHUNK:COLS].reshape(n_head, LANES),
            (((0,), (0,)), ((), ())),
            preferred_element_type=F32,
        ).astype(BF16)
        for i in range(blocks):
            rows_b[n_head:n_rows, i * LANES : (i + 1) * LANES] = low[i * n_tail : (i + 1) * n_tail, :]
        scaled_b[...] = (gcol[...] * rows_b[...].astype(F32)).astype(BF16)

        def partial(xx, inner):
            rows = pl.ds(pl.multiple_of(xx * xb_rows, xb_rows), xb_rows)
            out = mm(ht[rows, :], scaled_b[...]).astype(BF16)
            for cc in range(CORES):
                pb[c, cc, xx] = out[cc * piece : (cc + 1) * piece, :]
            return inner

        lax.fori_loop(0, xs, partial, 0)
        remote(pb.at[c, 1 - core], pr.at[c], pair_s.at[c], pair_r.at[c], mate)

        @pl.when(c == chunks - 1)
        def _():
            each(from_y, 0, chunks - 2)

        def accumulate(f, inner):
            rows = pl.ds(pl.multiple_of(f * fb, fb), fb)
            wcols = pl.ds(pl.multiple_of(c * CHUNK, CHUNK), CHUNK)
            proj[:, rows] += mm_nt(rows_b[...], w_v[rows, wcols])
            return inner

        lax.fori_loop(0, hidden // fb, accumulate, 0)

        await_bytes(pr.at[c], pair_r.at[c])
        for xx in range(xs):
            xb[c, xx] = (pb[c, core, xx].astype(F32) + pr[c, xx].astype(F32)).astype(BF16)
        for k in range(1, xs):
            remote(xb.at[c, lax.rem(x + k, xs)], xr.at[c, k - 1], x_s.at[c], x_r.at[c], xdev(k))

        @pl.when(c >= 1)
        def _():
            from_x(c - 1)

        return carry

    lax.fori_loop(0, chunks, main, 0)

    from_x(chunks - 1)
    each(from_y, chunks - 2, chunks)

    back_head, back_tail = order(HEAD, True), order(tail, True)

    def finish(f, score):
        cols = pl.ds(pl.multiple_of(f * fb, fb), fb)
        block = proj[:, cols]
        grad = (gcol[...] * block).astype(BF16)
        hg_v[0:n_head, cols] = mm(back_head, grad[0:n_head, :]).astype(BF16)
        hg_v[n_head:n_rows, cols] = mm(back_tail, grad[n_head:n_rows, :]).astype(BF16)
        return score + jnp.sum(block * hq[:, cols].astype(F32), axis=1, keepdims=True)

    score = lax.fori_loop(0, hidden // fb, finish, jnp.zeros((n_rows, 1), F32))
    srow = jnp.zeros((slots, LANES), F32)
    for per, base, first, _ in parts:
        n = slots * per
        collect = jnp.where(iota((1, n), 1) // per == iota((slots, n), 0), 1.0, 0.0)
        put = jnp.where(iota((n, LANES), 1) == rank_of(per, base), score[first : first + n, :], 0.0)
        srow = srow + lax.dot_general(
            collect, put, (((1,), (0,)), ((), ())), precision=lax.Precision.HIGHEST, preferred_element_type=F32
        )
    for s in range(slots):
        score_out[s] = srow[s : s + 1, :]

    def send_score(k, carry):
        remote(score_out.at[plane_slot(k)], score_in.at[e], score_s, score_r, plane(k))
        return carry

    lax.fori_loop(1, slots, send_score, 0)
    own_score = pltpu.make_async_copy(score_out.at[e], score_in.at[e], ld_sem.at[4])
    own_score.start()
    out_h = pltpu.make_async_copy(hg_v, hg_ref, ld_sem.at[5])
    out_h.start()

    each(from_z, 0, chunks)

    await_bytes(score_in.at[pl.ds(0, slots - 1)], score_r)
    own_score.wait()
    sin = score_in[:, 0, :]
    value = jnp.zeros((slots, toks), F32)
    for c in range(cap):
        value = jnp.where(rank == float(c), sin[:, c : c + 1], value)
    for k in range(topk):
        rg_ref[k : k + 1, :] = jnp.sum(jnp.where(match(k), value, 0.0), axis=0, keepdims=True)
    each(from_v, 0, chunks)
    each(from_w, 0, chunks)

    out_h.wait()
    await_bytes(gate_out.at[pl.ds(0, slots - 1)], gate_s)
    await_bytes(score_out.at[pl.ds(0, slots - 1)], score_s)

    def settle(c, carry):
        await_bytes(sbuf.at[c, pl.ds(0, slots - 1)], row_s.at[c])
        await_bytes(pr.at[c], pair_s.at[c])
        await_bytes(xr.at[c], x_s.at[c])
        await_bytes(yr.at[c], y_s.at[c])
        await_bytes(zr.at[c], z_s.at[c])
        await_bytes(zr.at[c], v_s.at[c])
        await_bytes(yr.at[c], w_s.at[c])
        return carry

    lax.fori_loop(0, chunks, settle, 0)


def local(groups, slots, out_grad, gates, routes, copy_pick, replica_plan, down_weight, saved_hidden):
    toks, width = out_grad.shape
    topk = routes.shape[1]
    hidden = down_weight.shape[1]
    cap = saved_hidden.shape[3]
    xs, zs = groups // CORES, slots // YS
    tail = cap - HEAD
    chunks = width // CHUNK
    n_rows = slots * cap
    n_head = slots * HEAD
    piece = hidden // groups
    zrows = piece // zs
    ycols = CHUNK // YS
    held = saved_hidden[0, 0].transpose(1, 0, 2).reshape(n_rows, hidden)
    vmem = pltpu.VMEM
    dma = pltpu.SemaphoreType.DMA
    scratch = [
        vmem((toks, width), BF16),
        vmem((hidden, width), BF16),
        vmem((n_rows, hidden), BF16),
        vmem((n_rows, hidden), BF16),
        vmem((hidden, n_rows), BF16),
        vmem((n_head, toks), BF16),
        vmem((slots * tail, toks), BF16),
        vmem((n_head, n_head), BF16),
        vmem((chunks, slots, HEAD, COLS), BF16),
        vmem((chunks, slots, HEAD, COLS), BF16),
        vmem((slots, 1, LANES), F32),
        vmem((slots, 1, LANES), F32),
        vmem((slots, 1, LANES), F32),
        vmem((slots, 1, LANES), F32),
        vmem((n_rows, CHUNK), BF16),
        vmem((n_rows, CHUNK), BF16),
        vmem((n_rows, 1), F32),
        vmem((n_rows, hidden), F32),
        vmem((n_rows, hidden), BF16),
        vmem((chunks, CORES, xs, piece, CHUNK), BF16),
        vmem((chunks, xs, piece, CHUNK), BF16),
        vmem((chunks, xs, piece, CHUNK), BF16),
        vmem((chunks, xs - 1, piece, CHUNK), BF16),
        vmem((chunks, YS, piece, ycols), BF16),
        vmem((chunks, YS - 1, piece, ycols), BF16),
        vmem((chunks, zs, 2, zrows, ycols), BF16),
        vmem((chunks, zs - 1, 2, zrows, ycols), BF16),
        vmem((chunks, 2, zrows, ycols), BF16),
        vmem((chunks, zs, 2, zrows, ycols), BF16),
        vmem((chunks, YS, piece, ycols), BF16),
        vmem((chunks, YS, piece, ycols), BF16),
        dma((6,)),
        dma((chunks,)),
        dma((chunks,)),
        dma((chunks,)),
        dma,
        dma,
        dma((chunks,)),
        dma((chunks,)),
        dma((chunks,)),
        dma((chunks,)),
        dma((chunks,)),
        dma((chunks,)),
        dma((chunks,)),
        dma((chunks,)),
        dma((chunks,)),
        dma((chunks,)),
        dma((chunks,)),
        dma((chunks,)),
        dma,
        dma,
    ]
    dims = (groups, slots, cap, toks, topk, width, hidden)
    here = pl.BlockSpec(memory_space=pltpu.VMEM)
    there = pl.BlockSpec(memory_space=pl.ANY)
    route_grad, hidden_grad, copy_grad = pl.pallas_call(
        functools.partial(kernel, dims),
        out_shape=(
            jax.ShapeDtypeStruct((topk, toks), F32),
            jax.ShapeDtypeStruct((n_rows, hidden), BF16),
            jax.ShapeDtypeStruct((piece, width), BF16),
        ),
        in_specs=[there, there, there, here, here, here, here],
        out_specs=(here, there, here),
        scratch_shapes=scratch,
        compiler_params=pltpu.CompilerParams(
            collective_id=0, has_side_effects=True, vmem_limit_bytes=63 * 2**20
        ),
        name="expert_backward",
    )(out_grad, down_weight[0], held, gates.T, routes.T, copy_pick.T, replica_plan[None, :])
    hidden_grad = hidden_grad.reshape(cap, slots, hidden).transpose(1, 0, 2)
    return route_grad.T, hidden_grad[None, None], copy_grad[None]


def solution(mesh):
    groups, slots = mesh.shape["group"], mesh.shape["expert"]
    placed = (
        P(("group", "expert"), None),
        P(("group", "expert"), None),
        P(("group", "expert"), None),
        P(("group", "expert"), None),
        P(),
        P("expert", None, None),
        P("group", "expert", None, None, None),
    )
    return jax.shard_map(
        functools.partial(local, groups, slots),
        mesh=mesh,
        in_specs=placed,
        out_specs=(
            P(("group", "expert"), None),
            P("group", "expert", None, None, None),
            P("expert", "group", None),
        ),
        check_vma=False,
    )
```

```python
import functools

import jax
import jax.numpy as jnp
from jax import lax
from jax.experimental import pallas as pl
from jax.experimental.pallas import tpu as pltpu
from jax.sharding import PartitionSpec as P

CORES = 2
YS = 4
LANES = 128
HEAD = 16
CHUNK = 512
COLS = CHUNK + LANES
MESH = pl.DeviceIdType.MESH
F32 = jnp.float32
BF16 = jnp.bfloat16


def iota(shape, dim):
    return lax.broadcasted_iota(jnp.int32, shape, dim)


def mm(a, b):
    return lax.dot_general(a, b, (((1,), (0,)), ((), ())), preferred_element_type=F32)


def mm_nt(a, b):
    return lax.dot_general(a, b, (((1,), (1,)), ((), ())), preferred_element_type=F32)


def onehot(mask):
    return jnp.where(mask, 1.0, 0.0).astype(BF16)


def kernel(
    dims,
    og_hbm,
    w_hbm,
    h_hbm,
    gates_ref,
    routes_ref,
    pick_ref,
    plan_ref,
    rg_ref,
    hg_ref,
    cg_ref,
    og_v,
    w_v,
    h_v,
    hq,
    ht,
    s_head,
    s_tail,
    shuffle,
    sbuf,
    rbuf,
    gate_out,
    gate_in,
    score_out,
    score_in,
    rows_b,
    scaled_b,
    gcol,
    proj,
    hg_v,
    pb,
    pr,
    xb,
    xr,
    gsum,
    yr,
    tb,
    zr,
    ub,
    vb,
    wb,
    ya,
    ld_sem,
    own_sem,
    row_s,
    row_r,
    gate_s,
    gate_r,
    pair_s,
    pair_r,
    x_s,
    x_r,
    y_s,
    y_r,
    z_s,
    z_r,
    v_s,
    v_r,
    w_s,
    w_r,
    score_s,
    score_r,
):
    groups, slots, cap, toks, topk, width, hidden = dims
    xs, zs = groups // CORES, slots // YS
    tail = cap - HEAD
    chunks = width // CHUNK
    n_head, n_tail = slots * HEAD, slots * tail
    n_rows = n_head + n_tail
    piece = hidden // groups
    zrows = piece // zs
    ycols = CHUNK // YS

    g = lax.axis_index("group")
    e = lax.axis_index("expert")
    x, core = g // CORES, g % CORES
    z, y = e // YS, e % YS
    mate = (x * CORES + (1 - core), e)

    def plane(k):
        return (g, lax.rem(z + k // YS, zs) * YS + lax.rem(y + k % YS, YS))

    def plane_slot(k):
        return lax.rem(z + k // YS, zs) * YS + lax.rem(y + k % YS, YS)

    def xdev(k):
        return (lax.rem(x + k, xs) * CORES + core, e)

    def ydev(k):
        return (g, z * YS + lax.rem(y + k, YS))

    def zdev(k):
        return (g, lax.rem(z + k, zs) * YS + y)

    def remote(src, dst, ssem, rsem, dev):
        pltpu.make_async_remote_copy(
            src_ref=src, dst_ref=dst, send_sem=ssem, recv_sem=rsem, device_id=dev, device_id_type=MESH
        ).start()

    def await_bytes(ref, sem):
        pltpu.make_async_copy(ref, ref, sem).wait()

    ld_og = pltpu.make_async_copy(og_hbm, og_v, ld_sem.at[0])
    ld_h = pltpu.make_async_copy(h_hbm, h_v, ld_sem.at[1])
    ld_w = pltpu.make_async_copy(w_hbm, w_v, ld_sem.at[2])
    ld_og.start()
    ld_h.start()
    ld_w.start()

    barrier = pltpu.get_barrier_semaphore()

    def greet(k, carry):
        pl.semaphore_signal(barrier, inc=1, device_id=plane(k), device_id_type=MESH)
        return carry

    lax.fori_loop(1, slots, greet, 0)
    pl.semaphore_signal(barrier, inc=1, device_id=mate, device_id_type=MESH)
    for k in range(1, xs):
        pl.semaphore_signal(barrier, inc=1, device_id=xdev(k), device_id_type=MESH)

    plan_row = plan_ref[...].astype(F32)
    si, ti = iota((slots, slots), 0), iota((slots, slots), 1)
    plan_col = jnp.sum(jnp.where(si == ti, plan_row, 0.0), axis=1, keepdims=True)
    same = jnp.where(plan_col == plan_row, 1.0, 0.0)
    reps_col = jnp.sum(same, axis=1, keepdims=True)
    reps_row = jnp.sum(same, axis=0, keepdims=True)
    ord_col = jnp.sum(jnp.where(ti < si, same, 0.0), axis=1, keepdims=True)
    ord_row = jnp.sum(jnp.where(si < ti, same, 0.0), axis=0, keepdims=True)
    first_row = jnp.where((reps_row > 1.0) & (ord_row == 0.0), 1.0, 0.0)
    hot_rank = jnp.sum(jnp.where(plan_row < plan_col, first_row, 0.0), axis=1, keepdims=True)
    slot_id = iota((slots, 1), 0)

    def at_slot(col, slot):
        return jnp.sum(jnp.where(slot_id == slot, col, 0.0), axis=0, keepdims=True)

    in_table = [jnp.where((reps_col > 1.0) & (hot_rank == float(h)), 1.0, 0.0) for h in range(2)]
    y_weight = [[at_slot(in_table[h], z * YS + yy) for h in range(2)] for yy in range(YS)]
    near_weight = [[at_slot(in_table[h], z * YS + lax.rem(y + YS - k, YS)) for h in range(2)] for k in range(YS)]
    my_hot = at_slot(in_table[0] + in_table[1], e) > 0.0

    inv_reps = 1.0 / reps_col

    def match(k):
        route = routes_ref[k : k + 1, :].astype(F32)
        pick = pick_ref[k : k + 1, :].astype(F32)
        chosen = pick - jnp.floor((pick + 0.5) * inv_reps) * reps_col
        return (plan_col == route) & (chosen == ord_col)

    taken = jnp.zeros((slots, toks), F32)
    gate_of = jnp.zeros((slots, toks), F32)
    for k in range(topk):
        hit = match(k)
        taken = jnp.where(hit, 1.0, taken)
        gate_of = jnp.where(hit, gates_ref[k : k + 1, :], gate_of)
    before = onehot(iota((toks, toks), 0) < iota((toks, toks), 1))
    rank = mm(taken.astype(BF16), before)
    rank = jnp.where((taken > 0.0) & (rank < float(cap)), rank, 64.0)
    rank_b, gate_b = rank.astype(BF16), gate_of.astype(BF16)
    parts = ((HEAD, 0, 0, s_head), (tail, HEAD, n_head, s_tail))

    def spread(per):
        n = slots * per
        return onehot(iota((n, 1), 0) // per == iota((n, slots), 1))

    def rank_of(per, base):
        return iota((slots * per, 1), 0) % per + base

    for per, base, _, s_ref in parts:
        s_ref[...] = onehot(mm(spread(per), rank_b) == rank_of(per, base).astype(F32))

    blocks = CHUNK // LANES
    rr = iota((n_head, 1), 0)
    shuffle[...] = onehot(
        iota((n_head, n_head), 1) == (rr // tail % blocks) * n_tail + (rr // HEAD) * tail + rr % tail
    )

    ld_og.wait()

    def gather(c):
        part = og_v[:, pl.ds(pl.multiple_of(c * CHUNK, CHUNK), CHUNK)]
        sbuf[c, :, :, 0:CHUNK] = mm(s_head[...], part).astype(BF16).reshape(slots, HEAD, CHUNK)
        low = mm(s_tail[...], part).astype(BF16)
        low = jnp.concatenate([low[:, i * LANES : (i + 1) * LANES] for i in range(blocks)], axis=0)
        sbuf[c, :, :, CHUNK:COLS] = mm(shuffle[...], low).astype(BF16).reshape(slots, HEAD, LANES)

    gather(0)
    pl.semaphore_wait(barrier, slots + xs - 1)

    def send_gate(k, carry):
        remote(gate_out.at[plane_slot(k)], gate_in.at[e], gate_s, gate_r, plane(k))
        return carry

    def dispatch(c, carry):
        def one(k, inner):
            remote(sbuf.at[c, plane_slot(k)], rbuf.at[c, e], row_s.at[c], row_r.at[c], plane(k))
            return inner

        lax.fori_loop(1, slots, one, 0)
        pltpu.make_async_copy(sbuf.at[c, e], rbuf.at[c, e], own_sem.at[c]).start()

        @pl.when(c + 1 < chunks)
        def _():
            gather(c + 1)

        return carry

    dispatch(0, 0)

    grow = jnp.zeros((slots, LANES), F32)
    for per, base, _, s_ref in parts:
        n = slots * per
        collect = onehot(iota((1, n), 1) // per == iota((slots, n), 0))
        held = jnp.sum(s_ref[...].astype(F32) * mm(spread(per), gate_b), axis=1, keepdims=True)
        put = jnp.where(iota((n, LANES), 1) == rank_of(per, base), held, 0.0)
        grow = grow + mm(collect, put.astype(BF16))
    for s in range(slots):
        gate_out[s] = grow[s : s + 1, :]
    lax.fori_loop(1, slots, send_gate, 0)
    own_gate = pltpu.make_async_copy(gate_out.at[e], gate_in.at[e], ld_sem.at[3])
    own_gate.start()
    lax.fori_loop(1, chunks, dispatch, 0)

    ld_h.wait()
    fb = min(256, hidden)

    def order(per, back):
        n = slots * per
        r, c = iota((n, 1), 0), iota((n, n), 1)
        if back:
            return onehot(c == (r % slots) * per + r // slots)
        return onehot(c == (r % per) * slots + r // per)

    fwd_head, fwd_tail = order(HEAD, False), order(tail, False)

    def reorder(f, carry):
        cols = pl.ds(pl.multiple_of(f * fb, fb), fb)
        hq[0:n_head, cols] = mm(fwd_head, h_v[0:n_head, cols]).astype(BF16)
        hq[n_head:n_rows, cols] = mm(fwd_tail, h_v[n_head:n_rows, cols]).astype(BF16)
        ht[cols, :] = hq[:, cols].T
        return carry

    lax.fori_loop(0, hidden // fb, reorder, 0)
    proj[...] = jnp.zeros_like(proj)

    await_bytes(gate_in.at[pl.ds(0, slots - 1)], gate_r)
    own_gate.wait()
    gin = gate_in[:, 0, :].astype(BF16)
    for per, base, first, _ in parts:
        n = slots * per
        picked = jnp.where(iota((n, LANES), 1) == rank_of(per, base), mm(spread(per), gin), 0.0)
        gcol[first : first + n, :] = jnp.sum(picked, axis=1, keepdims=True)
    ld_w.wait()
    xb_rows = CORES * piece

    def from_x(c):
        await_bytes(xr.at[c], x_r.at[c])
        total = xb[c, x].astype(F32)
        for k in range(xs - 1):
            total = total + xr[c, k].astype(F32)
        total = total.astype(BF16)
        for yy in range(YS):
            gsum[c, yy] = total[:, yy * ycols : (yy + 1) * ycols]
        for k in range(1, YS):
            remote(gsum.at[c, lax.rem(y + k, YS)], yr.at[c, k - 1], y_s.at[c], y_r.at[c], ydev(k))

    def from_y(c):
        await_bytes(yr.at[c], y_r.at[c])
        came = [gsum[c, y].astype(F32)] + [yr[c, k - 1].astype(F32) for k in range(1, YS)]
        for h in range(2):
            total = near_weight[0][h] * came[0]
            for k in range(1, YS):
                total = total + near_weight[k][h] * came[k]
            tb[c, :, h] = total.astype(BF16).reshape(zs, zrows, ycols)
        for k in range(1, zs):
            remote(tb.at[c, lax.rem(z + k, zs)], zr.at[c, k - 1], z_s.at[c], z_r.at[c], zdev(k))

    def from_z(c):
        await_bytes(zr.at[c], z_r.at[c])
        total = tb[c, z].astype(F32)
        for k in range(zs - 1):
            total = total + zr[c, k].astype(F32)
        total = total.astype(BF16)
        ub[c] = total
        vb[c, z] = total
        for k in range(1, zs):
            remote(ub.at[c], vb.at[c, z], v_s.at[c], v_r.at[c], zdev(k))

    def from_v(c):
        await_bytes(vb.at[c, pl.ds(0, zs - 1)], v_r.at[c])
        tables = [vb[c, :, h].reshape(piece, ycols).astype(F32) for h in range(2)]
        for yy in range(YS):
            wb[c, yy] = (y_weight[yy][0] * tables[0] + y_weight[yy][1] * tables[1]).astype(BF16)
        ya[c, y] = wb[c, y]
        for k in range(1, YS):
            remote(wb.at[c, lax.rem(y + k, YS)], ya.at[c, y], w_s.at[c], w_r.at[c], ydev(k))

    def from_w(c):
        await_bytes(ya.at[c, pl.ds(0, YS - 1)], w_r.at[c])
        for yy in range(YS):
            cols = pl.ds(pl.multiple_of(c * CHUNK + yy * ycols, ycols), ycols)
            cg_ref[:, cols] = jnp.where(my_hot, ya[c, yy].astype(F32), gsum[c, yy].astype(F32)).astype(BF16)

    def each(stage, start, stop):
        def run(c, carry):
            stage(c)
            return carry

        lax.fori_loop(start, stop, run, 0)

    def main(c, carry):
        await_bytes(rbuf.at[c, pl.ds(0, slots - 1)], row_r.at[c])
        pltpu.make_async_copy(sbuf.at[c, e], rbuf.at[c, e], own_sem.at[c]).wait()
        rows_b[0:n_head, :] = rbuf[c, :, :, 0:CHUNK].reshape(n_head, CHUNK)
        low = lax.dot_general(
            shuffle[...],
            rbuf[c, :, :, CHUNK:COLS].reshape(n_head, LANES),
            (((0,), (0,)), ((), ())),
            preferred_element_type=F32,
        ).astype(BF16)
        for i in range(blocks):
            rows_b[n_head:n_rows, i * LANES : (i + 1) * LANES] = low[i * n_tail : (i + 1) * n_tail, :]
        scaled_b[...] = (gcol[...] * rows_b[...].astype(F32)).astype(BF16)

        def partial(xx, inner):
            rows = pl.ds(pl.multiple_of(xx * xb_rows, xb_rows), xb_rows)
            out = mm(ht[rows, :], scaled_b[...]).astype(BF16)
            for cc in range(CORES):
                pb[c, cc, xx] = out[cc * piece : (cc + 1) * piece, :]
            return inner

        lax.fori_loop(0, xs, partial, 0)
        remote(pb.at[c, 1 - core], pr.at[c], pair_s.at[c], pair_r.at[c], mate)

        @pl.when(c == chunks - 1)
        def _():
            each(from_y, 0, chunks - 2)

        def accumulate(f, inner):
            rows = pl.ds(pl.multiple_of(f * fb, fb), fb)
            wcols = pl.ds(pl.multiple_of(c * CHUNK, CHUNK), CHUNK)
            proj[:, rows] += mm_nt(rows_b[...], w_v[rows, wcols])
            return inner

        lax.fori_loop(0, hidden // fb, accumulate, 0)

        await_bytes(pr.at[c], pair_r.at[c])
        for xx in range(xs):
            xb[c, xx] = (pb[c, core, xx].astype(F32) + pr[c, xx].astype(F32)).astype(BF16)
        for k in range(1, xs):
            remote(xb.at[c, lax.rem(x + k, xs)], xr.at[c, k - 1], x_s.at[c], x_r.at[c], xdev(k))

        @pl.when(c >= 1)
        def _():
            from_x(c - 1)

        return carry

    lax.fori_loop(0, chunks, main, 0)

    back_head, back_tail = order(HEAD, True), order(tail, True)

    def finish(f, score):
        cols = pl.ds(pl.multiple_of(f * fb, fb), fb)
        block = proj[:, cols]
        grad = (gcol[...] * block).astype(BF16)
        hg_v[0:n_head, cols] = mm(back_head, grad[0:n_head, :]).astype(BF16)
        hg_v[n_head:n_rows, cols] = mm(back_tail, grad[n_head:n_rows, :]).astype(BF16)
        return score + jnp.sum(block * hq[:, cols].astype(F32), axis=1, keepdims=True)

    score = lax.fori_loop(0, hidden // fb, finish, jnp.zeros((n_rows, 1), F32))
    srow = jnp.zeros((slots, LANES), F32)
    for per, base, first, _ in parts:
        n = slots * per
        collect = jnp.where(iota((1, n), 1) // per == iota((slots, n), 0), 1.0, 0.0)
        put = jnp.where(iota((n, LANES), 1) == rank_of(per, base), score[first : first + n, :], 0.0)
        srow = srow + lax.dot_general(
            collect, put, (((1,), (0,)), ((), ())), precision=lax.Precision.HIGHEST, preferred_element_type=F32
        )
    for s in range(slots):
        score_out[s] = srow[s : s + 1, :]

    def send_score(k, carry):
        remote(score_out.at[plane_slot(k)], score_in.at[e], score_s, score_r, plane(k))
        return carry

    lax.fori_loop(1, slots, send_score, 0)
    own_score = pltpu.make_async_copy(score_out.at[e], score_in.at[e], ld_sem.at[4])
    own_score.start()
    out_h = pltpu.make_async_copy(hg_v, hg_ref, ld_sem.at[5])
    out_h.start()

    each(from_y, chunks - 2, chunks - 1)
    each(from_z, 0, chunks - 2)
    from_x(chunks - 1)
    each(from_y, chunks - 1, chunks)
    each(from_z, chunks - 2, chunks)

    await_bytes(score_in.at[pl.ds(0, slots - 1)], score_r)
    own_score.wait()
    sin = score_in[:, 0, :]
    value = jnp.zeros((slots, toks), F32)
    for c in range(cap):
        value = jnp.where(rank == float(c), sin[:, c : c + 1], value)
    for k in range(topk):
        rg_ref[k : k + 1, :] = jnp.sum(jnp.where(match(k), value, 0.0), axis=0, keepdims=True)
    each(from_v, 0, chunks)
    each(from_w, 0, chunks)

    out_h.wait()
    await_bytes(gate_out.at[pl.ds(0, slots - 1)], gate_s)
    await_bytes(score_out.at[pl.ds(0, slots - 1)], score_s)

    def settle(c, carry):
        await_bytes(sbuf.at[c, pl.ds(0, slots - 1)], row_s.at[c])
        await_bytes(pr.at[c], pair_s.at[c])
        await_bytes(xr.at[c], x_s.at[c])
        await_bytes(yr.at[c], y_s.at[c])
        await_bytes(zr.at[c], z_s.at[c])
        await_bytes(zr.at[c], v_s.at[c])
        await_bytes(yr.at[c], w_s.at[c])
        return carry

    lax.fori_loop(0, chunks, settle, 0)


def emit(pieces, r_hbm, h_hbm, c_hbm, r_out, h_out, c_out, r_v, h_v, c_v, in_sem, out_sem):
    rows = h_v.shape[0] // pieces
    moves = [(r_hbm, r_v, r_out), (c_hbm, c_v, c_out)]
    for i in range(pieces):
        part = pl.ds(i * rows, rows)
        moves.append((h_hbm.at[part], h_v.at[part], h_out.at[part]))
    ins = [pltpu.make_async_copy(src, mid, in_sem.at[i]) for i, (src, mid, _) in enumerate(moves)]
    outs = [pltpu.make_async_copy(mid, dst, out_sem.at[i]) for i, (_, mid, dst) in enumerate(moves)]
    for one in ins:
        one.start()
    for first, then in zip(ins, outs):
        first.wait()
        then.start()
    for one in outs:
        one.wait()


def local(groups, slots, out_grad, gates, routes, copy_pick, replica_plan, down_weight, saved_hidden):
    toks, width = out_grad.shape
    topk = routes.shape[1]
    hidden = down_weight.shape[1]
    cap = saved_hidden.shape[3]
    xs, zs = groups // CORES, slots // YS
    tail = cap - HEAD
    chunks = width // CHUNK
    n_rows = slots * cap
    n_head = slots * HEAD
    piece = hidden // groups
    zrows = piece // zs
    ycols = CHUNK // YS
    held = saved_hidden[0, 0].transpose(1, 0, 2).reshape(n_rows, hidden)
    vmem = pltpu.VMEM
    dma = pltpu.SemaphoreType.DMA
    scratch = [
        vmem((toks, width), BF16),
        vmem((hidden, width), BF16),
        vmem((n_rows, hidden), BF16),
        vmem((n_rows, hidden), BF16),
        vmem((hidden, n_rows), BF16),
        vmem((n_head, toks), BF16),
        vmem((slots * tail, toks), BF16),
        vmem((n_head, n_head), BF16),
        vmem((chunks, slots, HEAD, COLS), BF16),
        vmem((chunks, slots, HEAD, COLS), BF16),
        vmem((slots, 1, LANES), F32),
        vmem((slots, 1, LANES), F32),
        vmem((slots, 1, LANES), F32),
        vmem((slots, 1, LANES), F32),
        vmem((n_rows, CHUNK), BF16),
        vmem((n_rows, CHUNK), BF16),
        vmem((n_rows, 1), F32),
        vmem((n_rows, hidden), F32),
        vmem((n_rows, hidden), BF16),
        vmem((chunks, CORES, xs, piece, CHUNK), BF16),
        vmem((chunks, xs, piece, CHUNK), BF16),
        vmem((chunks, xs, piece, CHUNK), BF16),
        vmem((chunks, xs - 1, piece, CHUNK), BF16),
        vmem((chunks, YS, piece, ycols), BF16),
        vmem((chunks, YS - 1, piece, ycols), BF16),
        vmem((chunks, zs, 2, zrows, ycols), BF16),
        vmem((chunks, zs - 1, 2, zrows, ycols), BF16),
        vmem((chunks, 2, zrows, ycols), BF16),
        vmem((chunks, zs, 2, zrows, ycols), BF16),
        vmem((chunks, YS, piece, ycols), BF16),
        vmem((chunks, YS, piece, ycols), BF16),
        dma((6,)),
        dma((chunks,)),
        dma((chunks,)),
        dma((chunks,)),
        dma,
        dma,
        dma((chunks,)),
        dma((chunks,)),
        dma((chunks,)),
        dma((chunks,)),
        dma((chunks,)),
        dma((chunks,)),
        dma((chunks,)),
        dma((chunks,)),
        dma((chunks,)),
        dma((chunks,)),
        dma((chunks,)),
        dma((chunks,)),
        dma,
        dma,
    ]
    dims = (groups, slots, cap, toks, topk, width, hidden)
    here = pl.BlockSpec(memory_space=pltpu.VMEM)
    there = pl.BlockSpec(memory_space=pl.ANY)
    route_grad, hidden_grad, copy_grad = pl.pallas_call(
        functools.partial(kernel, dims),
        out_shape=(
            jax.ShapeDtypeStruct((topk, toks), F32),
            jax.ShapeDtypeStruct((n_rows, hidden), BF16),
            jax.ShapeDtypeStruct((piece, width), BF16),
        ),
        in_specs=[there, there, there, here, here, here, here],
        out_specs=(here, there, here),
        scratch_shapes=scratch,
        compiler_params=pltpu.CompilerParams(
            collective_id=0, has_side_effects=True, vmem_limit_bytes=63 * 2**20
        ),
        name="expert_backward",
    )(out_grad, down_weight[0], held, gates.T, routes.T, copy_pick.T, replica_plan[None, :])
    shapes = (route_grad.shape, hidden_grad.shape, copy_grad.shape)
    kinds = (F32, BF16, BF16)
    pieces = 4
    route_grad, hidden_grad, copy_grad = pl.pallas_call(
        functools.partial(emit, pieces),
        out_shape=tuple(jax.ShapeDtypeStruct(s, k) for s, k in zip(shapes, kinds)),
        in_specs=[there, there, there],
        out_specs=(there, there, there),
        scratch_shapes=[vmem(s, k) for s, k in zip(shapes, kinds)] + [dma((pieces + 2,)), dma((pieces + 2,))],
        name="results",
    )(route_grad, hidden_grad, copy_grad)
    hidden_grad = hidden_grad.reshape(cap, slots, hidden).transpose(1, 0, 2)
    return route_grad.T, hidden_grad[None, None], copy_grad[None]


def solution(mesh):
    groups, slots = mesh.shape["group"], mesh.shape["expert"]
    placed = (
        P(("group", "expert"), None),
        P(("group", "expert"), None),
        P(("group", "expert"), None),
        P(("group", "expert"), None),
        P(),
        P("expert", None, None),
        P("group", "expert", None, None, None),
    )
    return jax.shard_map(
        functools.partial(local, groups, slots),
        mesh=mesh,
        in_specs=placed,
        out_specs=(
            P(("group", "expert"), None),
            P("group", "expert", None, None, None),
            P("expert", "group", None),
        ),
        check_vma=False,
    )
```

```python
import functools

import jax
import jax.numpy as jnp
from jax import lax
from jax.experimental import pallas as pl
from jax.experimental.pallas import tpu as pltpu
from jax.sharding import PartitionSpec as P

CORES = 2
YS = 4
LANES = 128
HEAD = 16
CHUNK = 512
COLS = CHUNK + LANES
PARTS = 1
HALF = CHUNK // PARTS
FIRST = 2
MESH = pl.DeviceIdType.MESH
F32 = jnp.float32
BF16 = jnp.bfloat16


def iota(shape, dim):
    return lax.broadcasted_iota(jnp.int32, shape, dim)


def mm(a, b):
    return lax.dot_general(a, b, (((1,), (0,)), ((), ())), preferred_element_type=F32)


def mm_nt(a, b):
    return lax.dot_general(a, b, (((1,), (1,)), ((), ())), preferred_element_type=F32)


def groups_of(chunks):
    cuts = [*range(0, chunks - 2, FIRST), chunks - 2, chunks - 1, chunks]
    return list(zip(cuts, cuts[1:]))


def onehot(mask):
    return jnp.where(mask, 1.0, 0.0).astype(BF16)


def kernel(
    dims,
    og_hbm,
    w_hbm,
    h_hbm,
    gates_ref,
    routes_ref,
    pick_ref,
    plan_ref,
    rg_ref,
    hg_ref,
    cg_ref,
    og_v,
    w_v,
    h_v,
    hq,
    ht,
    s_head,
    s_tail,
    shuffle,
    sbuf,
    rbuf,
    gate_out,
    gate_in,
    score_out,
    score_in,
    rows_b,
    scaled_b,
    low_b,
    gcol,
    proj,
    hg_v,
    pb,
    pr,
    xb,
    xr,
    gsum,
    yr,
    tb,
    zr,
    ub,
    vb,
    wb,
    ya,
    ld_sem,
    own_sem,
    row_s,
    row_r,
    gate_s,
    gate_r,
    pair_s,
    pair_r,
    x_s,
    x_r,
    y_s,
    y_r,
    z_s,
    z_r,
    v_s,
    v_r,
    w_s,
    w_r,
    score_s,
    score_r,
):
    groups, slots, cap, toks, topk, width, hidden = dims
    xs, zs = groups // CORES, slots // YS
    tail = cap - HEAD
    chunks = width // CHUNK
    n_head, n_tail = slots * HEAD, slots * tail
    n_rows = n_head + n_tail
    piece = hidden // groups
    zrows = piece // zs
    ycols = CHUNK // YS

    g = lax.axis_index("group")
    e = lax.axis_index("expert")
    x, core = g // CORES, g % CORES
    z, y = e // YS, e % YS
    mate = (x * CORES + (1 - core), e)

    def plane(k):
        return (g, lax.rem(z + k // YS, zs) * YS + lax.rem(y + k % YS, YS))

    def plane_slot(k):
        return lax.rem(z + k // YS, zs) * YS + lax.rem(y + k % YS, YS)

    def xdev(k):
        return (lax.rem(x + k, xs) * CORES + core, e)

    def ydev(k):
        return (g, z * YS + lax.rem(y + k, YS))

    def zdev(k):
        return (g, lax.rem(z + k, zs) * YS + y)

    def remote(src, dst, ssem, rsem, dev):
        pltpu.make_async_remote_copy(
            src_ref=src, dst_ref=dst, send_sem=ssem, recv_sem=rsem, device_id=dev, device_id_type=MESH
        ).start()

    def await_bytes(ref, sem):
        pltpu.make_async_copy(ref, ref, sem).wait()

    ld_og = pltpu.make_async_copy(og_hbm, og_v, ld_sem.at[0])
    ld_h = pltpu.make_async_copy(h_hbm, h_v, ld_sem.at[1])
    ld_w = pltpu.make_async_copy(w_hbm, w_v, ld_sem.at[2])
    ld_og.start()
    ld_h.start()
    ld_w.start()

    barrier = pltpu.get_barrier_semaphore()

    def greet(k, carry):
        pl.semaphore_signal(barrier, inc=1, device_id=plane(k), device_id_type=MESH)
        return carry

    lax.fori_loop(1, slots, greet, 0)
    pl.semaphore_signal(barrier, inc=1, device_id=mate, device_id_type=MESH)
    for k in range(1, xs):
        pl.semaphore_signal(barrier, inc=1, device_id=xdev(k), device_id_type=MESH)

    plan_row = plan_ref[...].astype(F32)
    si, ti = iota((slots, slots), 0), iota((slots, slots), 1)
    plan_col = jnp.sum(jnp.where(si == ti, plan_row, 0.0), axis=1, keepdims=True)
    same = jnp.where(plan_col == plan_row, 1.0, 0.0)
    reps_col = jnp.sum(same, axis=1, keepdims=True)
    reps_row = jnp.sum(same, axis=0, keepdims=True)
    ord_col = jnp.sum(jnp.where(ti < si, same, 0.0), axis=1, keepdims=True)
    ord_row = jnp.sum(jnp.where(si < ti, same, 0.0), axis=0, keepdims=True)
    first_row = jnp.where((reps_row > 1.0) & (ord_row == 0.0), 1.0, 0.0)
    hot_rank = jnp.sum(jnp.where(plan_row < plan_col, first_row, 0.0), axis=1, keepdims=True)
    slot_id = iota((slots, 1), 0)

    def at_slot(col, slot):
        return jnp.sum(jnp.where(slot_id == slot, col, 0.0), axis=0, keepdims=True)

    in_table = [jnp.where((reps_col > 1.0) & (hot_rank == float(h)), 1.0, 0.0) for h in range(2)]
    y_weight = [[at_slot(in_table[h], z * YS + yy) for h in range(2)] for yy in range(YS)]
    near_weight = [[at_slot(in_table[h], z * YS + lax.rem(y + YS - k, YS)) for h in range(2)] for k in range(YS)]
    my_hot = at_slot(in_table[0] + in_table[1], e) > 0.0

    inv_reps = 1.0 / reps_col

    def match(k):
        route = routes_ref[k : k + 1, :].astype(F32)
        pick = pick_ref[k : k + 1, :].astype(F32)
        chosen = pick - jnp.floor((pick + 0.5) * inv_reps) * reps_col
        return (plan_col == route) & (chosen == ord_col)

    taken = jnp.zeros((slots, toks), F32)
    gate_of = jnp.zeros((slots, toks), F32)
    for k in range(topk):
        hit = match(k)
        taken = jnp.where(hit, 1.0, taken)
        gate_of = jnp.where(hit, gates_ref[k : k + 1, :], gate_of)
    before = onehot(iota((toks, toks), 0) < iota((toks, toks), 1))
    rank = mm(taken.astype(BF16), before)
    rank = jnp.where((taken > 0.0) & (rank < float(cap)), rank, 64.0)
    rank_b, gate_b = rank.astype(BF16), gate_of.astype(BF16)
    parts = ((HEAD, 0, 0, s_head), (tail, HEAD, n_head, s_tail))

    def spread(per):
        n = slots * per
        return onehot(iota((n, 1), 0) // per == iota((n, slots), 1))

    def rank_of(per, base):
        return iota((slots * per, 1), 0) % per + base

    for per, base, _, s_ref in parts:
        s_ref[...] = onehot(mm(spread(per), rank_b) == rank_of(per, base).astype(F32))

    blocks = CHUNK // LANES
    rr = iota((n_head, 1), 0)
    shuffle[...] = onehot(
        iota((n_head, n_head), 1) == (rr // tail % blocks) * n_tail + (rr // HEAD) * tail + rr % tail
    )

    ld_og.wait()

    def gather(c):
        part = og_v[:, pl.ds(pl.multiple_of(c * CHUNK, CHUNK), CHUNK)]
        sbuf[c, :, :, 0:CHUNK] = mm(s_head[...], part).astype(BF16).reshape(slots, HEAD, CHUNK)
        low = mm(s_tail[...], part).astype(BF16)
        low = jnp.concatenate([low[:, i * LANES : (i + 1) * LANES] for i in range(blocks)], axis=0)
        sbuf[c, :, :, CHUNK:COLS] = mm(shuffle[...], low).astype(BF16).reshape(slots, HEAD, LANES)

    gather(0)
    pl.semaphore_wait(barrier, slots + xs - 1)

    def send_gate(k, carry):
        remote(gate_out.at[plane_slot(k)], gate_in.at[e], gate_s, gate_r, plane(k))
        return carry

    def dispatch(c, carry):
        def one(k, inner):
            remote(sbuf.at[c, plane_slot(k)], rbuf.at[c, e], row_s.at[c], row_r.at[c], plane(k))
            return inner

        lax.fori_loop(1, slots, one, 0)
        pltpu.make_async_copy(sbuf.at[c, e], rbuf.at[c, e], own_sem.at[c]).start()

        @pl.when(c + 1 < chunks)
        def _():
            gather(c + 1)

        return carry

    dispatch(0, 0)

    grow = jnp.zeros((slots, LANES), F32)
    for per, base, _, s_ref in parts:
        n = slots * per
        collect = onehot(iota((1, n), 1) // per == iota((slots, n), 0))
        held = jnp.sum(s_ref[...].astype(F32) * mm(spread(per), gate_b), axis=1, keepdims=True)
        put = jnp.where(iota((n, LANES), 1) == rank_of(per, base), held, 0.0)
        grow = grow + mm(collect, put.astype(BF16))
    for s in range(slots):
        gate_out[s] = grow[s : s + 1, :]
    lax.fori_loop(1, slots, send_gate, 0)
    own_gate = pltpu.make_async_copy(gate_out.at[e], gate_in.at[e], ld_sem.at[3])
    own_gate.start()
    lax.fori_loop(1, chunks, dispatch, 0)

    ld_h.wait()
    fb = min(256, hidden)

    def order(per, back):
        n = slots * per
        r, c = iota((n, 1), 0), iota((n, n), 1)
        if back:
            return onehot(c == (r % slots) * per + r // slots)
        return onehot(c == (r % per) * slots + r // per)

    fwd_head, fwd_tail = order(HEAD, False), order(tail, False)

    def reorder(f, carry):
        cols = pl.ds(pl.multiple_of(f * fb, fb), fb)
        hq[0:n_head, cols] = mm(fwd_head, h_v[0:n_head, cols]).astype(BF16)
        hq[n_head:n_rows, cols] = mm(fwd_tail, h_v[n_head:n_rows, cols]).astype(BF16)
        ht[cols, :] = hq[:, cols].T
        return carry

    lax.fori_loop(0, hidden // fb, reorder, 0)
    proj[...] = jnp.zeros_like(proj)

    await_bytes(gate_in.at[pl.ds(0, slots - 1)], gate_r)
    own_gate.wait()
    gin = gate_in[:, 0, :].astype(BF16)
    for per, base, first, _ in parts:
        n = slots * per
        picked = jnp.where(iota((n, LANES), 1) == rank_of(per, base), mm(spread(per), gin), 0.0)
        gcol[first : first + n, :] = jnp.sum(picked, axis=1, keepdims=True)
    ld_w.wait()
    xb_rows = CORES * piece

    def from_x(c, j):
        await_bytes(xr.at[c, j], x_r.at[c, j])
        total = xb[c, j, x].astype(F32)
        for k in range(xs - 1):
            total = total + xr[c, j, k].astype(F32)
        total = total.astype(BF16)
        for i in range(YS // PARTS):
            gsum[j * (YS // PARTS) + i, c] = total[:, i * ycols : (i + 1) * ycols]

    stages = [(i,) + span for i, span in enumerate(groups_of(chunks))]
    early = [stage for stage in stages if stage[2] <= chunks - 2]
    middle = [stage for stage in stages if stage[2] == chunks - 1]
    last = stages[-1]

    def each(stage, lo, hi):
        def run(c, carry):
            stage(c)
            return carry

        lax.fori_loop(lo, hi, run, 0)

    def to_y(i, lo, hi):
        span = pl.ds(lo, hi - lo)
        for k in range(1, YS):
            remote(gsum.at[lax.rem(y + k, YS), span], yr.at[k - 1, span], y_s.at[i], y_r.at[i], ydev(k))

    def from_y(i, lo, hi):
        span = pl.ds(lo, hi - lo)
        await_bytes(yr.at[:, span], y_r.at[i])

        def one(c):
            came = [gsum[y, c].astype(F32)] + [yr[k - 1, c].astype(F32) for k in range(1, YS)]
            for h in range(2):
                total = near_weight[0][h] * came[0]
                for k in range(1, YS):
                    total = total + near_weight[k][h] * came[k]
                tb[:, c, h] = total.astype(BF16).reshape(zs, zrows, ycols)

        each(one, lo, hi)
        for k in range(1, zs):
            remote(tb.at[lax.rem(z + k, zs), span], zr.at[k - 1, span], z_s.at[i], z_r.at[i], zdev(k))

    def from_z(i, lo, hi):
        span = pl.ds(lo, hi - lo)
        await_bytes(zr.at[:, span], z_r.at[i])

        def one(c):
            total = tb[z, c].astype(F32)
            for k in range(zs - 1):
                total = total + zr[k, c].astype(F32)
            total = total.astype(BF16)
            ub[c] = total
            vb[z, c] = total

        each(one, lo, hi)
        for k in range(1, zs):
            remote(ub.at[span], vb.at[z, span], v_s.at[i], v_r.at[i], zdev(k))

    def from_v(i, lo, hi):
        span = pl.ds(lo, hi - lo)
        await_bytes(vb.at[pl.ds(0, zs - 1), span], v_r.at[i])

        def one(c):
            tables = [vb[:, c, h].reshape(piece, ycols).astype(F32) for h in range(2)]
            for yy in range(YS):
                wb[yy, c] = (y_weight[yy][0] * tables[0] + y_weight[yy][1] * tables[1]).astype(BF16)
            ya[y, c] = wb[y, c]

        each(one, lo, hi)
        for k in range(1, YS):
            remote(wb.at[lax.rem(y + k, YS), span], ya.at[y, span], w_s.at[i], w_r.at[i], ydev(k))

    def from_w(i, lo, hi):
        span = pl.ds(lo, hi - lo)
        await_bytes(ya.at[pl.ds(0, YS - 1), span], w_r.at[i])

        def one(c):
            for yy in range(YS):
                cols = pl.ds(pl.multiple_of(c * CHUNK + yy * ycols, ycols), ycols)
                cg_ref[:, cols] = jnp.where(my_hot, ya[yy, c].astype(F32), gsum[yy, c].astype(F32)).astype(BF16)

        each(one, lo, hi)

    def main(c, carry):
        await_bytes(rbuf.at[c, pl.ds(0, slots - 1)], row_r.at[c])
        pltpu.make_async_copy(sbuf.at[c, e], rbuf.at[c, e], own_sem.at[c]).wait()
        low = lax.dot_general(
            shuffle[...],
            rbuf[c, :, :, CHUNK:COLS].reshape(n_head, LANES),
            (((0,), (0,)), ((), ())),
            preferred_element_type=F32,
        ).astype(BF16)
        for i in range(blocks):
            low_b[:, i * LANES : (i + 1) * LANES] = low[i * n_tail : (i + 1) * n_tail, :]
        for j in range(PARTS):
            cols = slice(j * HALF, (j + 1) * HALF)
            rows_b[0:n_head, cols] = rbuf[c, :, :, cols].reshape(n_head, HALF)
            rows_b[n_head:n_rows, cols] = low_b[:, cols]
            scaled_b[...] = (gcol[...] * rows_b[:, cols].astype(F32)).astype(BF16)

            def partial(xx, inner):
                rows = pl.ds(pl.multiple_of(xx * xb_rows, xb_rows), xb_rows)
                out = mm(ht[rows, :], scaled_b[...]).astype(BF16)
                for cc in range(CORES):
                    pb[c, j, cc, xx] = out[cc * piece : (cc + 1) * piece, :]
                return inner

            lax.fori_loop(0, xs, partial, 0)
            remote(pb.at[c, j, 1 - core], pr.at[c, j], pair_s.at[c, j], pair_r.at[c, j], mate)

        @pl.when(c == chunks - 1)
        def _():
            for stage in early:
                from_y(*stage)

        def accumulate(f, inner):
            rows = pl.ds(pl.multiple_of(f * fb, fb), fb)
            wcols = pl.ds(pl.multiple_of(c * CHUNK, CHUNK), CHUNK)
            proj[:, rows] += mm_nt(rows_b[...], w_v[rows, wcols])
            return inner

        lax.fori_loop(0, hidden // fb, accumulate, 0)

        for j in range(PARTS):
            await_bytes(pr.at[c, j], pair_r.at[c, j])
            for xx in range(xs):
                xb[c, j, xx] = (pb[c, j, core, xx].astype(F32) + pr[c, j, xx].astype(F32)).astype(BF16)
            for k in range(1, xs):
                remote(xb.at[c, j, lax.rem(x + k, xs)], xr.at[c, j, k - 1], x_s.at[c, j], x_r.at[c, j], xdev(k))

        @pl.when(c >= 1)
        def _():
            for j in range(PARTS):
                from_x(c - 1, j)

        for stage in early + middle:

            @pl.when(c == stage[2])
            def _():
                to_y(*stage)

        return carry

    lax.fori_loop(0, chunks, main, 0)

    back_head, back_tail = order(HEAD, True), order(tail, True)

    def finish(f, score):
        cols = pl.ds(pl.multiple_of(f * fb, fb), fb)
        block = proj[:, cols]
        grad = (gcol[...] * block).astype(BF16)
        hg_v[0:n_head, cols] = mm(back_head, grad[0:n_head, :]).astype(BF16)
        hg_v[n_head:n_rows, cols] = mm(back_tail, grad[n_head:n_rows, :]).astype(BF16)
        return score + jnp.sum(block * hq[:, cols].astype(F32), axis=1, keepdims=True)

    score = lax.fori_loop(0, hidden // fb, finish, jnp.zeros((n_rows, 1), F32))
    srow = jnp.zeros((slots, LANES), F32)
    for per, base, first, _ in parts:
        n = slots * per
        collect = jnp.where(iota((1, n), 1) // per == iota((slots, n), 0), 1.0, 0.0)
        put = jnp.where(iota((n, LANES), 1) == rank_of(per, base), score[first : first + n, :], 0.0)
        srow = srow + lax.dot_general(
            collect, put, (((1,), (0,)), ((), ())), precision=lax.Precision.HIGHEST, preferred_element_type=F32
        )
    for s in range(slots):
        score_out[s] = srow[s : s + 1, :]

    def send_score(k, carry):
        remote(score_out.at[plane_slot(k)], score_in.at[e], score_s, score_r, plane(k))
        return carry

    lax.fori_loop(1, slots, send_score, 0)
    own_score = pltpu.make_async_copy(score_out.at[e], score_in.at[e], ld_sem.at[4])
    own_score.start()
    out_h = pltpu.make_async_copy(hg_v, hg_ref, ld_sem.at[5])
    out_h.start()

    for stage in middle:
        from_y(*stage)
    for stage in early:
        from_z(*stage)
    for j in range(PARTS):
        from_x(chunks - 1, j)
    to_y(*last)
    for stage in early[:1]:
        from_v(*stage)
    from_y(*last)
    for stage in middle:
        from_z(*stage)
    for stage in early[1:]:
        from_v(*stage)
    from_z(*last)

    await_bytes(score_in.at[pl.ds(0, slots - 1)], score_r)
    own_score.wait()
    sin = score_in[:, 0, :]
    value = jnp.zeros((slots, toks), F32)
    for c in range(cap):
        value = jnp.where(rank == float(c), sin[:, c : c + 1], value)
    for k in range(topk):
        rg_ref[k : k + 1, :] = jnp.sum(jnp.where(match(k), value, 0.0), axis=0, keepdims=True)
    for stage in middle:
        from_v(*stage)
    for stage in early + middle:
        from_w(*stage)
    from_v(*last)
    from_w(*last)

    out_h.wait()
    await_bytes(gate_out.at[pl.ds(0, slots - 1)], gate_s)
    await_bytes(score_out.at[pl.ds(0, slots - 1)], score_s)

    def settle(c, carry):
        await_bytes(sbuf.at[c, pl.ds(0, slots - 1)], row_s.at[c])
        for j in range(PARTS):
            await_bytes(pr.at[c, j], pair_s.at[c, j])
            await_bytes(xr.at[c, j], x_s.at[c, j])
        return carry

    lax.fori_loop(0, chunks, settle, 0)
    for i, lo, hi in stages:
        span = pl.ds(lo, hi - lo)
        await_bytes(yr.at[:, span], y_s.at[i])
        await_bytes(zr.at[:, span], z_s.at[i])
        await_bytes(zr.at[:, span], v_s.at[i])
        await_bytes(yr.at[:, span], w_s.at[i])


def emit(pieces, r_hbm, h_hbm, c_hbm, r_out, h_out, c_out, r_v, h_v, c_v, in_sem, out_sem):
    rows = h_v.shape[0] // pieces
    moves = [(r_hbm, r_v, r_out), (c_hbm, c_v, c_out)]
    for i in range(pieces):
        part = pl.ds(i * rows, rows)
        moves.append((h_hbm.at[part], h_v.at[part], h_out.at[part]))
    ins = [pltpu.make_async_copy(src, mid, in_sem.at[i]) for i, (src, mid, _) in enumerate(moves)]
    outs = [pltpu.make_async_copy(mid, dst, out_sem.at[i]) for i, (_, mid, dst) in enumerate(moves)]
    for one in ins:
        one.start()
    for first, then in zip(ins, outs):
        first.wait()
        then.start()
    for one in outs:
        one.wait()


def local(groups, slots, out_grad, gates, routes, copy_pick, replica_plan, down_weight, saved_hidden):
    toks, width = out_grad.shape
    topk = routes.shape[1]
    hidden = down_weight.shape[1]
    cap = saved_hidden.shape[3]
    xs, zs = groups // CORES, slots // YS
    tail = cap - HEAD
    chunks = width // CHUNK
    n_rows = slots * cap
    n_head = slots * HEAD
    piece = hidden // groups
    zrows = piece // zs
    ycols = CHUNK // YS
    held = saved_hidden[0, 0].transpose(1, 0, 2).reshape(n_rows, hidden)
    vmem = pltpu.VMEM
    dma = pltpu.SemaphoreType.DMA
    scratch = [
        vmem((toks, width), BF16),
        vmem((hidden, width), BF16),
        vmem((n_rows, hidden), BF16),
        vmem((n_rows, hidden), BF16),
        vmem((hidden, n_rows), BF16),
        vmem((n_head, toks), BF16),
        vmem((slots * tail, toks), BF16),
        vmem((n_head, n_head), BF16),
        vmem((chunks, slots, HEAD, COLS), BF16),
        vmem((chunks, slots, HEAD, COLS), BF16),
        vmem((slots, 1, LANES), F32),
        vmem((slots, 1, LANES), F32),
        vmem((slots, 1, LANES), F32),
        vmem((slots, 1, LANES), F32),
        vmem((n_rows, CHUNK), BF16),
        vmem((n_rows, HALF), BF16),
        vmem((slots * tail, CHUNK), BF16),
        vmem((n_rows, 1), F32),
        vmem((n_rows, hidden), F32),
        vmem((n_rows, hidden), BF16),
        vmem((chunks, PARTS, CORES, xs, piece, HALF), BF16),
        vmem((chunks, PARTS, xs, piece, HALF), BF16),
        vmem((chunks, PARTS, xs, piece, HALF), BF16),
        vmem((chunks, PARTS, xs - 1, piece, HALF), BF16),
        vmem((YS, chunks, piece, ycols), BF16),
        vmem((YS - 1, chunks, piece, ycols), BF16),
        vmem((zs, chunks, 2, zrows, ycols), BF16),
        vmem((zs - 1, chunks, 2, zrows, ycols), BF16),
        vmem((chunks, 2, zrows, ycols), BF16),
        vmem((zs, chunks, 2, zrows, ycols), BF16),
        vmem((YS, chunks, piece, ycols), BF16),
        vmem((YS, chunks, piece, ycols), BF16),
        dma((6,)),
        dma((chunks,)),
        dma((chunks,)),
        dma((chunks,)),
        dma,
        dma,
        dma((chunks, PARTS)),
        dma((chunks, PARTS)),
        dma((chunks, PARTS)),
        dma((chunks, PARTS)),
        dma((len(groups_of(chunks)),)),
        dma((len(groups_of(chunks)),)),
        dma((len(groups_of(chunks)),)),
        dma((len(groups_of(chunks)),)),
        dma((len(groups_of(chunks)),)),
        dma((len(groups_of(chunks)),)),
        dma((len(groups_of(chunks)),)),
        dma((len(groups_of(chunks)),)),
        dma,
        dma,
    ]
    dims = (groups, slots, cap, toks, topk, width, hidden)
    here = pl.BlockSpec(memory_space=pltpu.VMEM)
    there = pl.BlockSpec(memory_space=pl.ANY)
    route_grad, hidden_grad, copy_grad = pl.pallas_call(
        functools.partial(kernel, dims),
        out_shape=(
            jax.ShapeDtypeStruct((topk, toks), F32),
            jax.ShapeDtypeStruct((n_rows, hidden), BF16),
            jax.ShapeDtypeStruct((piece, width), BF16),
        ),
        in_specs=[there, there, there, here, here, here, here],
        out_specs=(here, there, here),
        scratch_shapes=scratch,
        compiler_params=pltpu.CompilerParams(
            collective_id=0, has_side_effects=True, vmem_limit_bytes=63 * 2**20
        ),
        name="expert_backward",
    )(out_grad, down_weight[0], held, gates.T, routes.T, copy_pick.T, replica_plan[None, :])
    shapes = (route_grad.shape, hidden_grad.shape, copy_grad.shape)
    kinds = (F32, BF16, BF16)
    pieces = 4
    route_grad, hidden_grad, copy_grad = pl.pallas_call(
        functools.partial(emit, pieces),
        out_shape=tuple(jax.ShapeDtypeStruct(s, k) for s, k in zip(shapes, kinds)),
        in_specs=[there, there, there],
        out_specs=(there, there, there),
        scratch_shapes=[vmem(s, k) for s, k in zip(shapes, kinds)] + [dma((pieces + 2,)), dma((pieces + 2,))],
        name="results",
    )(route_grad, hidden_grad, copy_grad)
    hidden_grad = hidden_grad.reshape(cap, slots, hidden).transpose(1, 0, 2)
    return route_grad.T, hidden_grad[None, None], copy_grad[None]


def solution(mesh):
    groups, slots = mesh.shape["group"], mesh.shape["expert"]
    placed = (
        P(("group", "expert"), None),
        P(("group", "expert"), None),
        P(("group", "expert"), None),
        P(("group", "expert"), None),
        P(),
        P("expert", None, None),
        P("group", "expert", None, None, None),
    )
    return jax.shard_map(
        functools.partial(local, groups, slots),
        mesh=mesh,
        in_specs=placed,
        out_specs=(
            P(("group", "expert"), None),
            P("group", "expert", None, None, None),
            P("expert", "group", None),
        ),
        check_vma=False,
    )
```

```python
import functools

import jax
import jax.numpy as jnp
from jax import lax
from jax.experimental import pallas as pl
from jax.experimental.pallas import tpu as pltpu
from jax.sharding import PartitionSpec as P

CORES = 2
YS = 4
LANES = 128
HEAD = 16
CHUNK = 512
COLS = CHUNK + LANES
PARTS = 1
HALF = CHUNK // PARTS
FIRST = 2
MESH = pl.DeviceIdType.MESH
F32 = jnp.float32
BF16 = jnp.bfloat16


def iota(shape, dim):
    return lax.broadcasted_iota(jnp.int32, shape, dim)


def mm(a, b):
    return lax.dot_general(a, b, (((1,), (0,)), ((), ())), preferred_element_type=F32)


def mm_nt(a, b):
    return lax.dot_general(a, b, (((1,), (1,)), ((), ())), preferred_element_type=F32)


def groups_of(chunks):
    cuts = [*range(0, chunks - 2, FIRST), chunks - 2, chunks - 1, chunks]
    return list(zip(cuts, cuts[1:]))


def onehot(mask):
    return jnp.where(mask, 1.0, 0.0).astype(BF16)


def kernel(
    dims,
    og_hbm,
    w_hbm,
    h_hbm,
    gates_ref,
    routes_ref,
    pick_ref,
    plan_ref,
    rg_ref,
    hg_ref,
    cg_ref,
    og_v,
    w_v,
    h_v,
    hq,
    ht,
    s_head,
    s_tail,
    shuffle,
    sbuf,
    rbuf,
    gate_out,
    gate_in,
    score_out,
    score_in,
    rows_b,
    scaled_b,
    low_b,
    gcol,
    proj,
    pb,
    pr,
    xb,
    xr,
    gsum,
    yr,
    tb,
    zr,
    ub,
    vb,
    wb,
    ya,
    ld_sem,
    own_sem,
    row_s,
    row_r,
    gate_s,
    gate_r,
    pair_s,
    pair_r,
    x_s,
    x_r,
    y_s,
    y_r,
    z_s,
    z_r,
    v_s,
    v_r,
    w_s,
    w_r,
    score_s,
    score_r,
):
    groups, slots, cap, toks, topk, width, hidden = dims
    xs, zs = groups // CORES, slots // YS
    tail = cap - HEAD
    chunks = width // CHUNK
    n_head, n_tail = slots * HEAD, slots * tail
    n_rows = n_head + n_tail
    piece = hidden // groups
    zrows = piece // zs
    ycols = CHUNK // YS

    g = lax.axis_index("group")
    e = lax.axis_index("expert")
    x, core = g // CORES, g % CORES
    z, y = e // YS, e % YS
    mate = (x * CORES + (1 - core), e)

    def plane(k):
        return (g, lax.rem(z + k // YS, zs) * YS + lax.rem(y + k % YS, YS))

    def plane_slot(k):
        return lax.rem(z + k // YS, zs) * YS + lax.rem(y + k % YS, YS)

    def xdev(k):
        return (lax.rem(x + k, xs) * CORES + core, e)

    def ydev(k):
        return (g, z * YS + lax.rem(y + k, YS))

    def zdev(k):
        return (g, lax.rem(z + k, zs) * YS + y)

    def remote(src, dst, ssem, rsem, dev):
        pltpu.make_async_remote_copy(
            src_ref=src, dst_ref=dst, send_sem=ssem, recv_sem=rsem, device_id=dev, device_id_type=MESH
        ).start()

    def await_bytes(ref, sem):
        pltpu.make_async_copy(ref, ref, sem).wait()

    ld_og = pltpu.make_async_copy(og_hbm, og_v, ld_sem.at[0])
    ld_h = pltpu.make_async_copy(h_hbm, h_v, ld_sem.at[1])
    ld_w = pltpu.make_async_copy(w_hbm, w_v, ld_sem.at[2])
    ld_og.start()
    ld_h.start()
    ld_w.start()

    barrier = pltpu.get_barrier_semaphore()

    def greet(k, carry):
        pl.semaphore_signal(barrier, inc=1, device_id=plane(k), device_id_type=MESH)
        return carry

    lax.fori_loop(1, slots, greet, 0)
    pl.semaphore_signal(barrier, inc=1, device_id=mate, device_id_type=MESH)
    for k in range(1, xs):
        pl.semaphore_signal(barrier, inc=1, device_id=xdev(k), device_id_type=MESH)

    plan_row = plan_ref[...].astype(F32)
    si, ti = iota((slots, slots), 0), iota((slots, slots), 1)
    plan_col = jnp.sum(jnp.where(si == ti, plan_row, 0.0), axis=1, keepdims=True)
    same = jnp.where(plan_col == plan_row, 1.0, 0.0)
    reps_col = jnp.sum(same, axis=1, keepdims=True)
    reps_row = jnp.sum(same, axis=0, keepdims=True)
    ord_col = jnp.sum(jnp.where(ti < si, same, 0.0), axis=1, keepdims=True)
    ord_row = jnp.sum(jnp.where(si < ti, same, 0.0), axis=0, keepdims=True)
    first_row = jnp.where((reps_row > 1.0) & (ord_row == 0.0), 1.0, 0.0)
    hot_rank = jnp.sum(jnp.where(plan_row < plan_col, first_row, 0.0), axis=1, keepdims=True)
    slot_id = iota((slots, 1), 0)

    def at_slot(col, slot):
        return jnp.sum(jnp.where(slot_id == slot, col, 0.0), axis=0, keepdims=True)

    in_table = [jnp.where((reps_col > 1.0) & (hot_rank == float(h)), 1.0, 0.0) for h in range(2)]
    y_weight = [[at_slot(in_table[h], z * YS + yy) for h in range(2)] for yy in range(YS)]
    near_weight = [[at_slot(in_table[h], z * YS + lax.rem(y + YS - k, YS)) for h in range(2)] for k in range(YS)]
    my_hot = at_slot(in_table[0] + in_table[1], e) > 0.0

    inv_reps = 1.0 / reps_col

    def match(k):
        route = routes_ref[k : k + 1, :].astype(F32)
        pick = pick_ref[k : k + 1, :].astype(F32)
        chosen = pick - jnp.floor((pick + 0.5) * inv_reps) * reps_col
        return (plan_col == route) & (chosen == ord_col)

    taken = jnp.zeros((slots, toks), F32)
    gate_of = jnp.zeros((slots, toks), F32)
    for k in range(topk):
        hit = match(k)
        taken = jnp.where(hit, 1.0, taken)
        gate_of = jnp.where(hit, gates_ref[k : k + 1, :], gate_of)
    before = onehot(iota((toks, toks), 0) < iota((toks, toks), 1))
    rank = mm(taken.astype(BF16), before)
    rank = jnp.where((taken > 0.0) & (rank < float(cap)), rank, 64.0)
    rank_b, gate_b = rank.astype(BF16), gate_of.astype(BF16)
    parts = ((HEAD, 0, 0, s_head), (tail, HEAD, n_head, s_tail))

    def spread(per):
        n = slots * per
        return onehot(iota((n, 1), 0) // per == iota((n, slots), 1))

    def rank_of(per, base):
        return iota((slots * per, 1), 0) % per + base

    for per, base, _, s_ref in parts:
        s_ref[...] = onehot(mm(spread(per), rank_b) == rank_of(per, base).astype(F32))

    blocks = CHUNK // LANES
    rr = iota((n_head, 1), 0)
    shuffle[...] = onehot(
        iota((n_head, n_head), 1) == (rr // tail % blocks) * n_tail + (rr // HEAD) * tail + rr % tail
    )

    ld_og.wait()

    def gather(c):
        part = og_v[:, pl.ds(pl.multiple_of(c * CHUNK, CHUNK), CHUNK)]
        sbuf[c, :, :, 0:CHUNK] = mm(s_head[...], part).astype(BF16).reshape(slots, HEAD, CHUNK)
        low = mm(s_tail[...], part).astype(BF16)
        low = jnp.concatenate([low[:, i * LANES : (i + 1) * LANES] for i in range(blocks)], axis=0)
        sbuf[c, :, :, CHUNK:COLS] = mm(shuffle[...], low).astype(BF16).reshape(slots, HEAD, LANES)

    gather(0)
    pl.semaphore_wait(barrier, slots + xs - 1)

    def send_gate(k, carry):
        remote(gate_out.at[plane_slot(k)], gate_in.at[e], gate_s, gate_r, plane(k))
        return carry

    def dispatch(c, carry):
        def one(k, inner):
            remote(sbuf.at[c, plane_slot(k)], rbuf.at[c, e], row_s.at[c], row_r.at[c], plane(k))
            return inner

        lax.fori_loop(1, slots, one, 0)
        pltpu.make_async_copy(sbuf.at[c, e], rbuf.at[c, e], own_sem.at[c]).start()

        @pl.when(c + 1 < chunks)
        def _():
            gather(c + 1)

        return carry

    dispatch(0, 0)

    grow = jnp.zeros((slots, LANES), F32)
    for per, base, _, s_ref in parts:
        n = slots * per
        collect = onehot(iota((1, n), 1) // per == iota((slots, n), 0))
        held = jnp.sum(s_ref[...].astype(F32) * mm(spread(per), gate_b), axis=1, keepdims=True)
        put = jnp.where(iota((n, LANES), 1) == rank_of(per, base), held, 0.0)
        grow = grow + mm(collect, put.astype(BF16))
    for s in range(slots):
        gate_out[s] = grow[s : s + 1, :]
    lax.fori_loop(1, slots, send_gate, 0)
    own_gate = pltpu.make_async_copy(gate_out.at[e], gate_in.at[e], ld_sem.at[3])
    own_gate.start()
    lax.fori_loop(1, chunks, dispatch, 0)

    ld_h.wait()
    fb = min(256, hidden)

    def order(per, back):
        n = slots * per
        r, c = iota((n, 1), 0), iota((n, n), 1)
        if back:
            return onehot(c == (r % slots) * per + r // slots)
        return onehot(c == (r % per) * slots + r // per)

    fwd_head, fwd_tail = order(HEAD, False), order(tail, False)

    def reorder(f, carry):
        cols = pl.ds(pl.multiple_of(f * fb, fb), fb)
        hq[0:n_head, cols] = mm(fwd_head, h_v[0:n_head, cols]).astype(BF16)
        hq[n_head:n_rows, cols] = mm(fwd_tail, h_v[n_head:n_rows, cols]).astype(BF16)
        ht[cols, :] = hq[:, cols].T
        return carry

    lax.fori_loop(0, hidden // fb, reorder, 0)
    proj[...] = jnp.zeros_like(proj)

    await_bytes(gate_in.at[pl.ds(0, slots - 1)], gate_r)
    own_gate.wait()
    gin = gate_in[:, 0, :].astype(BF16)
    for per, base, first, _ in parts:
        n = slots * per
        picked = jnp.where(iota((n, LANES), 1) == rank_of(per, base), mm(spread(per), gin), 0.0)
        gcol[first : first + n, :] = jnp.sum(picked, axis=1, keepdims=True)
    ld_w.wait()
    xb_rows = CORES * piece

    def from_x(c, j):
        await_bytes(xr.at[c, j], x_r.at[c, j])
        total = xb[c, j, x].astype(F32)
        for k in range(xs - 1):
            total = total + xr[c, j, k].astype(F32)
        total = total.astype(BF16)
        for i in range(YS // PARTS):
            gsum[j * (YS // PARTS) + i, c] = total[:, i * ycols : (i + 1) * ycols]

    stages = [(i,) + span for i, span in enumerate(groups_of(chunks))]
    early = [stage for stage in stages if stage[2] <= chunks - 2]
    middle = [stage for stage in stages if stage[2] == chunks - 1]
    last = stages[-1]

    def each(stage, lo, hi):
        def run(c, carry):
            stage(c)
            return carry

        lax.fori_loop(lo, hi, run, 0)

    def to_y(i, lo, hi):
        span = pl.ds(lo, hi - lo)
        for k in range(1, YS):
            remote(gsum.at[lax.rem(y + k, YS), span], yr.at[k - 1, span], y_s.at[i], y_r.at[i], ydev(k))

    def from_y(i, lo, hi):
        span = pl.ds(lo, hi - lo)
        await_bytes(yr.at[:, span], y_r.at[i])

        def one(c):
            came = [gsum[y, c].astype(F32)] + [yr[k - 1, c].astype(F32) for k in range(1, YS)]
            for h in range(2):
                total = near_weight[0][h] * came[0]
                for k in range(1, YS):
                    total = total + near_weight[k][h] * came[k]
                tb[:, c, h] = total.astype(BF16).reshape(zs, zrows, ycols)

        each(one, lo, hi)
        for k in range(1, zs):
            remote(tb.at[lax.rem(z + k, zs), span], zr.at[k - 1, span], z_s.at[i], z_r.at[i], zdev(k))

    def from_z(i, lo, hi):
        span = pl.ds(lo, hi - lo)
        await_bytes(zr.at[:, span], z_r.at[i])

        def one(c):
            total = tb[z, c].astype(F32)
            for k in range(zs - 1):
                total = total + zr[k, c].astype(F32)
            total = total.astype(BF16)
            ub[c] = total
            vb[z, c] = total

        each(one, lo, hi)
        for k in range(1, zs):
            remote(ub.at[span], vb.at[z, span], v_s.at[i], v_r.at[i], zdev(k))

    def from_v(i, lo, hi):
        span = pl.ds(lo, hi - lo)
        await_bytes(vb.at[pl.ds(0, zs - 1), span], v_r.at[i])

        def one(c):
            tables = [vb[:, c, h].reshape(piece, ycols).astype(F32) for h in range(2)]
            for yy in range(YS):
                wb[yy, c] = (y_weight[yy][0] * tables[0] + y_weight[yy][1] * tables[1]).astype(BF16)
            ya[y, c] = wb[y, c]

        each(one, lo, hi)
        for k in range(1, YS):
            remote(wb.at[lax.rem(y + k, YS), span], ya.at[y, span], w_s.at[i], w_r.at[i], ydev(k))

    def from_w(i, lo, hi):
        span = pl.ds(lo, hi - lo)
        await_bytes(ya.at[pl.ds(0, YS - 1), span], w_r.at[i])

        def one(c):
            for yy in range(YS):
                cols = pl.ds(pl.multiple_of(c * CHUNK + yy * ycols, ycols), ycols)
                cg_ref[:, cols] = jnp.where(my_hot, ya[yy, c].astype(F32), gsum[yy, c].astype(F32)).astype(BF16)

        each(one, lo, hi)

    def main(c, carry):
        await_bytes(rbuf.at[c, pl.ds(0, slots - 1)], row_r.at[c])
        pltpu.make_async_copy(sbuf.at[c, e], rbuf.at[c, e], own_sem.at[c]).wait()
        low = lax.dot_general(
            shuffle[...],
            rbuf[c, :, :, CHUNK:COLS].reshape(n_head, LANES),
            (((0,), (0,)), ((), ())),
            preferred_element_type=F32,
        ).astype(BF16)
        for i in range(blocks):
            low_b[:, i * LANES : (i + 1) * LANES] = low[i * n_tail : (i + 1) * n_tail, :]
        for j in range(PARTS):
            cols = slice(j * HALF, (j + 1) * HALF)
            rows_b[0:n_head, cols] = rbuf[c, :, :, cols].reshape(n_head, HALF)
            rows_b[n_head:n_rows, cols] = low_b[:, cols]
            scaled_b[...] = (gcol[...] * rows_b[:, cols].astype(F32)).astype(BF16)

            def partial(xx, inner):
                rows = pl.ds(pl.multiple_of(xx * xb_rows, xb_rows), xb_rows)
                out = mm(ht[rows, :], scaled_b[...]).astype(BF16)
                for cc in range(CORES):
                    pb[c, j, cc, xx] = out[cc * piece : (cc + 1) * piece, :]
                return inner

            lax.fori_loop(0, xs, partial, 0)
            remote(pb.at[c, j, 1 - core], pr.at[c, j], pair_s.at[c, j], pair_r.at[c, j], mate)

        @pl.when(c == chunks - 1)
        def _():
            for stage in early:
                from_y(*stage)

        def accumulate(f, inner):
            rows = pl.ds(pl.multiple_of(f * fb, fb), fb)
            wcols = pl.ds(pl.multiple_of(c * CHUNK, CHUNK), CHUNK)
            proj[:, rows] += mm_nt(rows_b[...], w_v[rows, wcols])
            return inner

        lax.fori_loop(0, hidden // fb, accumulate, 0)

        for j in range(PARTS):
            await_bytes(pr.at[c, j], pair_r.at[c, j])
            for xx in range(xs):
                xb[c, j, xx] = (pb[c, j, core, xx].astype(F32) + pr[c, j, xx].astype(F32)).astype(BF16)
            for k in range(1, xs):
                remote(xb.at[c, j, lax.rem(x + k, xs)], xr.at[c, j, k - 1], x_s.at[c, j], x_r.at[c, j], xdev(k))

        @pl.when(c >= 1)
        def _():
            for j in range(PARTS):
                from_x(c - 1, j)

        for stage in early + middle:

            @pl.when(c == stage[2])
            def _():
                to_y(*stage)

        return carry

    lax.fori_loop(0, chunks, main, 0)

    back_head, back_tail = order(HEAD, True), order(tail, True)

    def finish(f, score):
        cols = pl.ds(pl.multiple_of(f * fb, fb), fb)
        block = proj[:, cols]
        grad = (gcol[...] * block).astype(BF16)
        hg_ref[0:n_head, cols] = mm(back_head, grad[0:n_head, :]).astype(BF16)
        hg_ref[n_head:n_rows, cols] = mm(back_tail, grad[n_head:n_rows, :]).astype(BF16)
        return score + jnp.sum(block * hq[:, cols].astype(F32), axis=1, keepdims=True)

    score = lax.fori_loop(0, hidden // fb, finish, jnp.zeros((n_rows, 1), F32))
    srow = jnp.zeros((slots, LANES), F32)
    for per, base, first, _ in parts:
        n = slots * per
        collect = jnp.where(iota((1, n), 1) // per == iota((slots, n), 0), 1.0, 0.0)
        put = jnp.where(iota((n, LANES), 1) == rank_of(per, base), score[first : first + n, :], 0.0)
        srow = srow + lax.dot_general(
            collect, put, (((1,), (0,)), ((), ())), precision=lax.Precision.HIGHEST, preferred_element_type=F32
        )
    for s in range(slots):
        score_out[s] = srow[s : s + 1, :]

    def send_score(k, carry):
        remote(score_out.at[plane_slot(k)], score_in.at[e], score_s, score_r, plane(k))
        return carry

    lax.fori_loop(1, slots, send_score, 0)
    own_score = pltpu.make_async_copy(score_out.at[e], score_in.at[e], ld_sem.at[4])
    own_score.start()

    for stage in middle:
        from_y(*stage)
    for stage in early:
        from_z(*stage)
    for j in range(PARTS):
        from_x(chunks - 1, j)
    to_y(*last)
    for stage in early[:1]:
        from_v(*stage)
    from_y(*last)
    for stage in middle:
        from_z(*stage)
    for stage in early[1:]:
        from_v(*stage)
    from_z(*last)

    await_bytes(score_in.at[pl.ds(0, slots - 1)], score_r)
    own_score.wait()
    sin = score_in[:, 0, :]
    value = jnp.zeros((slots, toks), F32)
    for c in range(cap):
        value = jnp.where(rank == float(c), sin[:, c : c + 1], value)
    for k in range(topk):
        rg_ref[k : k + 1, :] = jnp.sum(jnp.where(match(k), value, 0.0), axis=0, keepdims=True)
    for stage in middle:
        from_v(*stage)
    for stage in early + middle:
        from_w(*stage)
    from_v(*last)
    from_w(*last)

    await_bytes(gate_out.at[pl.ds(0, slots - 1)], gate_s)
    await_bytes(score_out.at[pl.ds(0, slots - 1)], score_s)

    def settle(c, carry):
        await_bytes(sbuf.at[c, pl.ds(0, slots - 1)], row_s.at[c])
        for j in range(PARTS):
            await_bytes(pr.at[c, j], pair_s.at[c, j])
            await_bytes(xr.at[c, j], x_s.at[c, j])
        return carry

    lax.fori_loop(0, chunks, settle, 0)
    for i, lo, hi in stages:
        span = pl.ds(lo, hi - lo)
        await_bytes(yr.at[:, span], y_s.at[i])
        await_bytes(zr.at[:, span], z_s.at[i])
        await_bytes(zr.at[:, span], v_s.at[i])
        await_bytes(yr.at[:, span], w_s.at[i])


def emit(r_v, h_v, c_v, r_out, h_out, c_out, sem):
    moves = [
        pltpu.make_async_copy(src, dst, sem.at[i])
        for i, (src, dst) in enumerate(((h_v, h_out), (c_v, c_out), (r_v, r_out)))
    ]
    for one in moves:
        one.start()
    for one in moves:
        one.wait()


def local(groups, slots, out_grad, gates, routes, copy_pick, replica_plan, down_weight, saved_hidden):
    toks, width = out_grad.shape
    topk = routes.shape[1]
    hidden = down_weight.shape[1]
    cap = saved_hidden.shape[3]
    xs, zs = groups // CORES, slots // YS
    tail = cap - HEAD
    chunks = width // CHUNK
    n_rows = slots * cap
    n_head = slots * HEAD
    piece = hidden // groups
    zrows = piece // zs
    ycols = CHUNK // YS
    held = saved_hidden[0, 0].transpose(1, 0, 2).reshape(n_rows, hidden)
    vmem = pltpu.VMEM
    dma = pltpu.SemaphoreType.DMA
    scratch = [
        vmem((toks, width), BF16),
        vmem((hidden, width), BF16),
        vmem((n_rows, hidden), BF16),
        vmem((n_rows, hidden), BF16),
        vmem((hidden, n_rows), BF16),
        vmem((n_head, toks), BF16),
        vmem((slots * tail, toks), BF16),
        vmem((n_head, n_head), BF16),
        vmem((chunks, slots, HEAD, COLS), BF16),
        vmem((chunks, slots, HEAD, COLS), BF16),
        vmem((slots, 1, LANES), F32),
        vmem((slots, 1, LANES), F32),
        vmem((slots, 1, LANES), F32),
        vmem((slots, 1, LANES), F32),
        vmem((n_rows, CHUNK), BF16),
        vmem((n_rows, HALF), BF16),
        vmem((slots * tail, CHUNK), BF16),
        vmem((n_rows, 1), F32),
        vmem((n_rows, hidden), F32),
        vmem((chunks, PARTS, CORES, xs, piece, HALF), BF16),
        vmem((chunks, PARTS, xs, piece, HALF), BF16),
        vmem((chunks, PARTS, xs, piece, HALF), BF16),
        vmem((chunks, PARTS, xs - 1, piece, HALF), BF16),
        vmem((YS, chunks, piece, ycols), BF16),
        vmem((YS - 1, chunks, piece, ycols), BF16),
        vmem((zs, chunks, 2, zrows, ycols), BF16),
        vmem((zs - 1, chunks, 2, zrows, ycols), BF16),
        vmem((chunks, 2, zrows, ycols), BF16),
        vmem((zs, chunks, 2, zrows, ycols), BF16),
        vmem((YS, chunks, piece, ycols), BF16),
        vmem((YS, chunks, piece, ycols), BF16),
        dma((6,)),
        dma((chunks,)),
        dma((chunks,)),
        dma((chunks,)),
        dma,
        dma,
        dma((chunks, PARTS)),
        dma((chunks, PARTS)),
        dma((chunks, PARTS)),
        dma((chunks, PARTS)),
        dma((len(groups_of(chunks)),)),
        dma((len(groups_of(chunks)),)),
        dma((len(groups_of(chunks)),)),
        dma((len(groups_of(chunks)),)),
        dma((len(groups_of(chunks)),)),
        dma((len(groups_of(chunks)),)),
        dma((len(groups_of(chunks)),)),
        dma((len(groups_of(chunks)),)),
        dma,
        dma,
    ]
    dims = (groups, slots, cap, toks, topk, width, hidden)
    here = pl.BlockSpec(memory_space=pltpu.VMEM)
    there = pl.BlockSpec(memory_space=pl.ANY)
    route_grad, hidden_grad, copy_grad = pl.pallas_call(
        functools.partial(kernel, dims),
        out_shape=(vmem((topk, toks), F32), vmem((n_rows, hidden), BF16), vmem((piece, width), BF16)),
        in_specs=[there, there, there, here, here, here, here],
        out_specs=(here, here, here),
        scratch_shapes=scratch,
        compiler_params=pltpu.CompilerParams(
            collective_id=0, has_side_effects=True, vmem_limit_bytes=58 * 2**20
        ),
        name="expert_backward",
    )(out_grad, down_weight[0], held, gates.T, routes.T, copy_pick.T, replica_plan[None, :])
    shapes = (route_grad.shape, hidden_grad.shape, copy_grad.shape)
    kinds = (F32, BF16, BF16)
    route_grad, hidden_grad, copy_grad = pl.pallas_call(
        emit,
        out_shape=tuple(jax.ShapeDtypeStruct(s, k) for s, k in zip(shapes, kinds)),
        in_specs=[here, here, here],
        out_specs=(there, there, there),
        scratch_shapes=[dma((3,))],
        name="results",
    )(*[pltpu.with_memory_space_constraint(a, pltpu.VMEM) for a in (route_grad, hidden_grad, copy_grad)])
    hidden_grad = hidden_grad.reshape(cap, slots, hidden).transpose(1, 0, 2)
    return route_grad.T, hidden_grad[None, None], copy_grad[None]


def solution(mesh):
    groups, slots = mesh.shape["group"], mesh.shape["expert"]
    placed = (
        P(("group", "expert"), None),
        P(("group", "expert"), None),
        P(("group", "expert"), None),
        P(("group", "expert"), None),
        P(),
        P("expert", None, None),
        P("group", "expert", None, None, None),
    )
    return jax.shard_map(
        functools.partial(local, groups, slots),
        mesh=mesh,
        in_specs=placed,
        out_specs=(
            P(("group", "expert"), None),
            P("group", "expert", None, None, None),
            P("expert", "group", None),
        ),
        check_vma=False,
    )
```

```python
import functools

import jax
import jax.numpy as jnp
from jax import lax
from jax.experimental import pallas as pl
from jax.experimental.pallas import tpu as pltpu
from jax.sharding import PartitionSpec as P

CORES = 2
YS = 4
LANES = 128
HEAD = 16
CHUNK = 512
COLS = CHUNK + LANES
PARTS = 1
HALF = CHUNK // PARTS
FIRST = 2
MESH = pl.DeviceIdType.MESH
F32 = jnp.float32
BF16 = jnp.bfloat16


def iota(shape, dim):
    return lax.broadcasted_iota(jnp.int32, shape, dim)


def mm(a, b):
    return lax.dot_general(a, b, (((1,), (0,)), ((), ())), preferred_element_type=F32)


def mm_nt(a, b):
    return lax.dot_general(a, b, (((1,), (1,)), ((), ())), preferred_element_type=F32)


def groups_of(chunks):
    cuts = [*range(0, chunks - 2, FIRST), chunks - 2, chunks - 1, chunks]
    return list(zip(cuts, cuts[1:]))


def onehot(mask):
    return jnp.where(mask, 1.0, 0.0).astype(BF16)


def kernel(
    dims,
    og_hbm,
    w_hbm,
    h_hbm,
    gates_ref,
    routes_ref,
    pick_ref,
    plan_ref,
    rg_ref,
    hg_ref,
    cg_ref,
    og_v,
    w_v,
    h_v,
    hq,
    ht,
    s_head,
    s_tail,
    shuffle,
    sbuf,
    rbuf,
    gate_out,
    gate_in,
    score_out,
    score_in,
    rows_b,
    scaled_b,
    low_b,
    gcol,
    proj,
    pb,
    pr,
    xb,
    xr,
    gsum,
    yr,
    tb,
    zr,
    ub,
    vb,
    wb,
    ya,
    ld_sem,
    own_sem,
    row_s,
    row_r,
    gate_s,
    gate_r,
    pair_s,
    pair_r,
    x_s,
    x_r,
    y_s,
    y_r,
    z_s,
    z_r,
    v_s,
    v_r,
    w_s,
    w_r,
    score_s,
    score_r,
):
    groups, slots, cap, toks, topk, width, hidden = dims
    xs, zs = groups // CORES, slots // YS
    tail = cap - HEAD
    chunks = width // CHUNK
    n_head, n_tail = slots * HEAD, slots * tail
    n_rows = n_head + n_tail
    piece = hidden // groups
    zrows = piece // zs
    ycols = CHUNK // YS

    g = lax.axis_index("group")
    e = lax.axis_index("expert")
    x, core = g // CORES, g % CORES
    z, y = e // YS, e % YS
    mate = (x * CORES + (1 - core), e)

    def plane(k):
        return (g, lax.rem(z + k // YS, zs) * YS + lax.rem(y + k % YS, YS))

    def plane_slot(k):
        return lax.rem(z + k // YS, zs) * YS + lax.rem(y + k % YS, YS)

    def xdev(k):
        return (lax.rem(x + k, xs) * CORES + core, e)

    def ydev(k):
        return (g, z * YS + lax.rem(y + k, YS))

    def zdev(k):
        return (g, lax.rem(z + k, zs) * YS + y)

    def remote(src, dst, ssem, rsem, dev):
        pltpu.make_async_remote_copy(
            src_ref=src, dst_ref=dst, send_sem=ssem, recv_sem=rsem, device_id=dev, device_id_type=MESH
        ).start()

    def await_bytes(ref, sem):
        pltpu.make_async_copy(ref, ref, sem).wait()

    ld_og = pltpu.make_async_copy(og_hbm, og_v, ld_sem.at[0])
    ld_h = pltpu.make_async_copy(h_hbm, h_v, ld_sem.at[1])
    ld_w = pltpu.make_async_copy(w_hbm, w_v, ld_sem.at[2])
    ld_og.start()
    ld_h.start()
    ld_w.start()

    barrier = pltpu.get_barrier_semaphore()

    def greet(k, carry):
        pl.semaphore_signal(barrier, inc=1, device_id=plane(k), device_id_type=MESH)
        return carry

    lax.fori_loop(1, slots, greet, 0)
    pl.semaphore_signal(barrier, inc=1, device_id=mate, device_id_type=MESH)
    for k in range(1, xs):
        pl.semaphore_signal(barrier, inc=1, device_id=xdev(k), device_id_type=MESH)

    plan_row = plan_ref[...].astype(F32)
    si, ti = iota((slots, slots), 0), iota((slots, slots), 1)
    plan_col = jnp.sum(jnp.where(si == ti, plan_row, 0.0), axis=1, keepdims=True)
    same = jnp.where(plan_col == plan_row, 1.0, 0.0)
    reps_col = jnp.sum(same, axis=1, keepdims=True)
    reps_row = jnp.sum(same, axis=0, keepdims=True)
    ord_col = jnp.sum(jnp.where(ti < si, same, 0.0), axis=1, keepdims=True)
    ord_row = jnp.sum(jnp.where(si < ti, same, 0.0), axis=0, keepdims=True)
    first_row = jnp.where((reps_row > 1.0) & (ord_row == 0.0), 1.0, 0.0)
    hot_rank = jnp.sum(jnp.where(plan_row < plan_col, first_row, 0.0), axis=1, keepdims=True)
    slot_id = iota((slots, 1), 0)

    def at_slot(col, slot):
        return jnp.sum(jnp.where(slot_id == slot, col, 0.0), axis=0, keepdims=True)

    in_table = [jnp.where((reps_col > 1.0) & (hot_rank == float(h)), 1.0, 0.0) for h in range(2)]
    y_weight = [[at_slot(in_table[h], z * YS + yy) for h in range(2)] for yy in range(YS)]
    near_weight = [[at_slot(in_table[h], z * YS + lax.rem(y + YS - k, YS)) for h in range(2)] for k in range(YS)]
    my_hot = at_slot(in_table[0] + in_table[1], e) > 0.0

    inv_reps = 1.0 / reps_col

    def match(k):
        route = routes_ref[k : k + 1, :].astype(F32)
        pick = pick_ref[k : k + 1, :].astype(F32)
        chosen = pick - jnp.floor((pick + 0.5) * inv_reps) * reps_col
        return (plan_col == route) & (chosen == ord_col)

    taken = jnp.zeros((slots, toks), F32)
    gate_of = jnp.zeros((slots, toks), F32)
    for k in range(topk):
        hit = match(k)
        taken = jnp.where(hit, 1.0, taken)
        gate_of = jnp.where(hit, gates_ref[k : k + 1, :], gate_of)
    before = onehot(iota((toks, toks), 0) < iota((toks, toks), 1))
    rank = mm(taken.astype(BF16), before)
    rank = jnp.where((taken > 0.0) & (rank < float(cap)), rank, 64.0)
    rank_b, gate_b = rank.astype(BF16), gate_of.astype(BF16)
    parts = ((HEAD, 0, 0, s_head), (tail, HEAD, n_head, s_tail))

    def spread(per):
        n = slots * per
        return onehot(iota((n, 1), 0) // per == iota((n, slots), 1))

    def rank_of(per, base):
        return iota((slots * per, 1), 0) % per + base

    for per, base, _, s_ref in parts:
        s_ref[...] = onehot(mm(spread(per), rank_b) == rank_of(per, base).astype(F32))

    blocks = CHUNK // LANES
    rr = iota((n_head, 1), 0)
    shuffle[...] = onehot(
        iota((n_head, n_head), 1) == (rr // tail % blocks) * n_tail + (rr // HEAD) * tail + rr % tail
    )

    ld_og.wait()

    def gather(c):
        part = og_v[:, pl.ds(pl.multiple_of(c * CHUNK, CHUNK), CHUNK)]
        sbuf[c, :, :, 0:CHUNK] = mm(s_head[...], part).astype(BF16).reshape(slots, HEAD, CHUNK)
        low = mm(s_tail[...], part).astype(BF16)
        low = jnp.concatenate([low[:, i * LANES : (i + 1) * LANES] for i in range(blocks)], axis=0)
        sbuf[c, :, :, CHUNK:COLS] = mm(shuffle[...], low).astype(BF16).reshape(slots, HEAD, LANES)

    gather(0)
    pl.semaphore_wait(barrier, slots + xs - 1)

    def send_gate(k, carry):
        remote(gate_out.at[plane_slot(k)], gate_in.at[e], gate_s, gate_r, plane(k))
        return carry

    def dispatch(c, carry):
        def one(k, inner):
            remote(sbuf.at[c, plane_slot(k)], rbuf.at[c, e], row_s.at[c], row_r.at[c], plane(k))
            return inner

        lax.fori_loop(1, slots, one, 0)
        pltpu.make_async_copy(sbuf.at[c, e], rbuf.at[c, e], own_sem.at[c]).start()

        @pl.when(c + 1 < chunks)
        def _():
            gather(c + 1)

        return carry

    dispatch(0, 0)

    grow = jnp.zeros((slots, LANES), F32)
    for per, base, _, s_ref in parts:
        n = slots * per
        collect = onehot(iota((1, n), 1) // per == iota((slots, n), 0))
        held = jnp.sum(s_ref[...].astype(F32) * mm(spread(per), gate_b), axis=1, keepdims=True)
        put = jnp.where(iota((n, LANES), 1) == rank_of(per, base), held, 0.0)
        grow = grow + mm(collect, put.astype(BF16))
    for s in range(slots):
        gate_out[s] = grow[s : s + 1, :]
    lax.fori_loop(1, slots, send_gate, 0)
    own_gate = pltpu.make_async_copy(gate_out.at[e], gate_in.at[e], ld_sem.at[3])
    own_gate.start()
    lax.fori_loop(1, chunks, dispatch, 0)

    ld_h.wait()
    fb = min(256, hidden)

    def order(per, back):
        n = slots * per
        r, c = iota((n, 1), 0), iota((n, n), 1)
        if back:
            return onehot(c == (r % slots) * per + r // slots)
        return onehot(c == (r % per) * slots + r // per)

    fwd_head, fwd_tail = order(HEAD, False), order(tail, False)

    def reorder(f, carry):
        cols = pl.ds(pl.multiple_of(f * fb, fb), fb)
        hq[0:n_head, cols] = mm(fwd_head, h_v[0:n_head, cols]).astype(BF16)
        hq[n_head:n_rows, cols] = mm(fwd_tail, h_v[n_head:n_rows, cols]).astype(BF16)
        ht[cols, :] = hq[:, cols].T
        return carry

    lax.fori_loop(0, hidden // fb, reorder, 0)
    proj[...] = jnp.zeros_like(proj)

    await_bytes(gate_in.at[pl.ds(0, slots - 1)], gate_r)
    own_gate.wait()
    gin = gate_in[:, 0, :].astype(BF16)
    for per, base, first, _ in parts:
        n = slots * per
        picked = jnp.where(iota((n, LANES), 1) == rank_of(per, base), mm(spread(per), gin), 0.0)
        gcol[first : first + n, :] = jnp.sum(picked, axis=1, keepdims=True)
    ld_w.wait()
    xb_rows = CORES * piece

    def from_x(c, j):
        await_bytes(xr.at[c, j], x_r.at[c, j])
        total = xb[c, j, x].astype(F32)
        for k in range(xs - 1):
            total = total + xr[c, j, k].astype(F32)
        total = total.astype(BF16)
        for i in range(YS // PARTS):
            gsum[j * (YS // PARTS) + i, c] = total[:, i * ycols : (i + 1) * ycols]

    stages = [(i,) + span for i, span in enumerate(groups_of(chunks))]
    early = [stage for stage in stages if stage[2] <= chunks - 2]
    middle = [stage for stage in stages if stage[2] == chunks - 1]
    last = stages[-1]

    def each(stage, lo, hi):
        def run(c, carry):
            stage(c)
            return carry

        lax.fori_loop(lo, hi, run, 0)

    def to_y(i, lo, hi):
        span = pl.ds(lo, hi - lo)
        for k in range(1, YS):
            remote(gsum.at[lax.rem(y + k, YS), span], yr.at[k - 1, span], y_s.at[i], y_r.at[i], ydev(k))

    def from_y(i, lo, hi):
        span = pl.ds(lo, hi - lo)
        await_bytes(yr.at[:, span], y_r.at[i])

        def one(c):
            came = [gsum[y, c].astype(F32)] + [yr[k - 1, c].astype(F32) for k in range(1, YS)]
            for h in range(2):
                total = near_weight[0][h] * came[0]
                for k in range(1, YS):
                    total = total + near_weight[k][h] * came[k]
                tb[:, c, h] = total.astype(BF16).reshape(zs, zrows, ycols)

        each(one, lo, hi)
        for k in range(1, zs):
            remote(tb.at[lax.rem(z + k, zs), span], zr.at[k - 1, span], z_s.at[i], z_r.at[i], zdev(k))

    def from_z(i, lo, hi):
        span = pl.ds(lo, hi - lo)
        await_bytes(zr.at[:, span], z_r.at[i])

        def one(c):
            total = tb[z, c].astype(F32)
            for k in range(zs - 1):
                total = total + zr[k, c].astype(F32)
            total = total.astype(BF16)
            ub[c] = total
            vb[z, c] = total

        each(one, lo, hi)
        for k in range(1, zs):
            remote(ub.at[span], vb.at[z, span], v_s.at[i], v_r.at[i], zdev(k))

    def from_v(i, lo, hi):
        span = pl.ds(lo, hi - lo)
        await_bytes(vb.at[pl.ds(0, zs - 1), span], v_r.at[i])

        def one(c):
            tables = [vb[:, c, h].reshape(piece, ycols).astype(F32) for h in range(2)]
            for yy in range(YS):
                wb[yy, c] = (y_weight[yy][0] * tables[0] + y_weight[yy][1] * tables[1]).astype(BF16)
            ya[y, c] = wb[y, c]

        each(one, lo, hi)
        for k in range(1, YS):
            remote(wb.at[lax.rem(y + k, YS), span], ya.at[y, span], w_s.at[i], w_r.at[i], ydev(k))

    def from_w(i, lo, hi):
        span = pl.ds(lo, hi - lo)
        await_bytes(ya.at[pl.ds(0, YS - 1), span], w_r.at[i])

        def one(c):
            for yy in range(YS):
                cols = pl.ds(pl.multiple_of(c * CHUNK + yy * ycols, ycols), ycols)
                cg_ref[:, cols] = jnp.where(my_hot, ya[yy, c].astype(F32), gsum[yy, c].astype(F32)).astype(BF16)

        each(one, lo, hi)

    def main(c, carry):
        await_bytes(rbuf.at[c, pl.ds(0, slots - 1)], row_r.at[c])
        pltpu.make_async_copy(sbuf.at[c, e], rbuf.at[c, e], own_sem.at[c]).wait()
        low = lax.dot_general(
            shuffle[...],
            rbuf[c, :, :, CHUNK:COLS].reshape(n_head, LANES),
            (((0,), (0,)), ((), ())),
            preferred_element_type=F32,
        ).astype(BF16)
        for i in range(blocks):
            low_b[:, i * LANES : (i + 1) * LANES] = low[i * n_tail : (i + 1) * n_tail, :]
        for j in range(PARTS):
            cols = slice(j * HALF, (j + 1) * HALF)
            rows_b[0:n_head, cols] = rbuf[c, :, :, cols].reshape(n_head, HALF)
            rows_b[n_head:n_rows, cols] = low_b[:, cols]
            scaled_b[...] = (gcol[...] * rows_b[:, cols].astype(F32)).astype(BF16)

            def partial(xx, inner):
                rows = pl.ds(pl.multiple_of(xx * xb_rows, xb_rows), xb_rows)
                out = mm(ht[rows, :], scaled_b[...]).astype(BF16)
                for cc in range(CORES):
                    pb[c, j, cc, xx] = out[cc * piece : (cc + 1) * piece, :]
                return inner

            lax.fori_loop(0, xs, partial, 0)
            remote(pb.at[c, j, 1 - core], pr.at[c, j], pair_s.at[c, j], pair_r.at[c, j], mate)

        @pl.when(c == chunks - 1)
        def _():
            for stage in early:
                from_y(*stage)

        def accumulate(f, inner):
            rows = pl.ds(pl.multiple_of(f * fb, fb), fb)
            wcols = pl.ds(pl.multiple_of(c * CHUNK, CHUNK), CHUNK)
            proj[:, rows] += mm_nt(rows_b[...], w_v[rows, wcols])
            return inner

        lax.fori_loop(0, hidden // fb, accumulate, 0)

        for j in range(PARTS):
            await_bytes(pr.at[c, j], pair_r.at[c, j])
            for xx in range(xs):
                xb[c, j, xx] = (pb[c, j, core, xx].astype(F32) + pr[c, j, xx].astype(F32)).astype(BF16)
            for k in range(1, xs):
                remote(xb.at[c, j, lax.rem(x + k, xs)], xr.at[c, j, k - 1], x_s.at[c, j], x_r.at[c, j], xdev(k))

        @pl.when(c >= 1)
        def _():
            for j in range(PARTS):
                from_x(c - 1, j)

        for stage in early + middle:

            @pl.when(c == stage[2])
            def _():
                to_y(*stage)

        return carry

    lax.fori_loop(0, chunks, main, 0)

    back_head, back_tail = order(HEAD, True), order(tail, True)

    def finish(f, score):
        cols = pl.ds(pl.multiple_of(f * fb, fb), fb)
        block = proj[:, cols]
        grad = (gcol[...] * block).astype(BF16)
        hg_ref[0:n_head, cols] = mm(back_head, grad[0:n_head, :]).astype(BF16)
        hg_ref[n_head:n_rows, cols] = mm(back_tail, grad[n_head:n_rows, :]).astype(BF16)
        return score + jnp.sum(block * hq[:, cols].astype(F32), axis=1, keepdims=True)

    score = lax.fori_loop(0, hidden // fb, finish, jnp.zeros((n_rows, 1), F32))
    srow = jnp.zeros((slots, LANES), F32)
    for per, base, first, _ in parts:
        n = slots * per
        collect = jnp.where(iota((1, n), 1) // per == iota((slots, n), 0), 1.0, 0.0)
        put = jnp.where(iota((n, LANES), 1) == rank_of(per, base), score[first : first + n, :], 0.0)
        srow = srow + lax.dot_general(
            collect, put, (((1,), (0,)), ((), ())), precision=lax.Precision.HIGHEST, preferred_element_type=F32
        )
    for s in range(slots):
        score_out[s] = srow[s : s + 1, :]

    def send_score(k, carry):
        remote(score_out.at[plane_slot(k)], score_in.at[e], score_s, score_r, plane(k))
        return carry

    for stage in middle:
        from_y(*stage)
    for j in range(PARTS):
        from_x(chunks - 1, j)
    to_y(*last)
    for stage in early:
        from_z(*stage)
    lax.fori_loop(1, slots, send_score, 0)
    own_score = pltpu.make_async_copy(score_out.at[e], score_in.at[e], ld_sem.at[4])
    own_score.start()
    for stage in early[:1]:
        from_v(*stage)
    from_y(*last)
    for stage in middle:
        from_z(*stage)
    for stage in early[1:]:
        from_v(*stage)
    from_z(*last)

    await_bytes(score_in.at[pl.ds(0, slots - 1)], score_r)
    own_score.wait()
    sin = score_in[:, 0, :]
    value = jnp.zeros((slots, toks), F32)
    for c in range(cap):
        value = jnp.where(rank == float(c), sin[:, c : c + 1], value)
    for k in range(topk):
        rg_ref[k : k + 1, :] = jnp.sum(jnp.where(match(k), value, 0.0), axis=0, keepdims=True)
    for stage in middle:
        from_v(*stage)
    for stage in early + middle:
        from_w(*stage)
    from_v(*last)
    from_w(*last)

    await_bytes(gate_out.at[pl.ds(0, slots - 1)], gate_s)
    await_bytes(score_out.at[pl.ds(0, slots - 1)], score_s)

    def settle(c, carry):
        await_bytes(sbuf.at[c, pl.ds(0, slots - 1)], row_s.at[c])
        for j in range(PARTS):
            await_bytes(pr.at[c, j], pair_s.at[c, j])
            await_bytes(xr.at[c, j], x_s.at[c, j])
        return carry

    lax.fori_loop(0, chunks, settle, 0)
    for i, lo, hi in stages:
        span = pl.ds(lo, hi - lo)
        await_bytes(yr.at[:, span], y_s.at[i])
        await_bytes(zr.at[:, span], z_s.at[i])
        await_bytes(zr.at[:, span], v_s.at[i])
        await_bytes(yr.at[:, span], w_s.at[i])


def emit(r_v, h_v, c_v, r_out, h_out, c_out, sem):
    moves = [
        pltpu.make_async_copy(src, dst, sem.at[i])
        for i, (src, dst) in enumerate(((h_v, h_out), (c_v, c_out), (r_v, r_out)))
    ]
    for one in moves:
        one.start()
    for one in moves:
        one.wait()


def local(groups, slots, out_grad, gates, routes, copy_pick, replica_plan, down_weight, saved_hidden):
    toks, width = out_grad.shape
    topk = routes.shape[1]
    hidden = down_weight.shape[1]
    cap = saved_hidden.shape[3]
    xs, zs = groups // CORES, slots // YS
    tail = cap - HEAD
    chunks = width // CHUNK
    n_rows = slots * cap
    n_head = slots * HEAD
    piece = hidden // groups
    zrows = piece // zs
    ycols = CHUNK // YS
    held = saved_hidden[0, 0].transpose(1, 0, 2).reshape(n_rows, hidden)
    vmem = pltpu.VMEM
    dma = pltpu.SemaphoreType.DMA
    scratch = [
        vmem((toks, width), BF16),
        vmem((hidden, width), BF16),
        vmem((n_rows, hidden), BF16),
        vmem((n_rows, hidden), BF16),
        vmem((hidden, n_rows), BF16),
        vmem((n_head, toks), BF16),
        vmem((slots * tail, toks), BF16),
        vmem((n_head, n_head), BF16),
        vmem((chunks, slots, HEAD, COLS), BF16),
        vmem((chunks, slots, HEAD, COLS), BF16),
        vmem((slots, 1, LANES), F32),
        vmem((slots, 1, LANES), F32),
        vmem((slots, 1, LANES), F32),
        vmem((slots, 1, LANES), F32),
        vmem((n_rows, CHUNK), BF16),
        vmem((n_rows, HALF), BF16),
        vmem((slots * tail, CHUNK), BF16),
        vmem((n_rows, 1), F32),
        vmem((n_rows, hidden), F32),
        vmem((chunks, PARTS, CORES, xs, piece, HALF), BF16),
        vmem((chunks, PARTS, xs, piece, HALF), BF16),
        vmem((chunks, PARTS, xs, piece, HALF), BF16),
        vmem((chunks, PARTS, xs - 1, piece, HALF), BF16),
        vmem((YS, chunks, piece, ycols), BF16),
        vmem((YS - 1, chunks, piece, ycols), BF16),
        vmem((zs, chunks, 2, zrows, ycols), BF16),
        vmem((zs - 1, chunks, 2, zrows, ycols), BF16),
        vmem((chunks, 2, zrows, ycols), BF16),
        vmem((zs, chunks, 2, zrows, ycols), BF16),
        vmem((YS, chunks, piece, ycols), BF16),
        vmem((YS, chunks, piece, ycols), BF16),
        dma((6,)),
        dma((chunks,)),
        dma((chunks,)),
        dma((chunks,)),
        dma,
        dma,
        dma((chunks, PARTS)),
        dma((chunks, PARTS)),
        dma((chunks, PARTS)),
        dma((chunks, PARTS)),
        dma((len(groups_of(chunks)),)),
        dma((len(groups_of(chunks)),)),
        dma((len(groups_of(chunks)),)),
        dma((len(groups_of(chunks)),)),
        dma((len(groups_of(chunks)),)),
        dma((len(groups_of(chunks)),)),
        dma((len(groups_of(chunks)),)),
        dma((len(groups_of(chunks)),)),
        dma,
        dma,
    ]
    dims = (groups, slots, cap, toks, topk, width, hidden)
    here = pl.BlockSpec(memory_space=pltpu.VMEM)
    there = pl.BlockSpec(memory_space=pl.ANY)
    route_grad, hidden_grad, copy_grad = pl.pallas_call(
        functools.partial(kernel, dims),
        out_shape=(vmem((topk, toks), F32), vmem((n_rows, hidden), BF16), vmem((piece, width), BF16)),
        in_specs=[there, there, there, here, here, here, here],
        out_specs=(here, here, here),
        scratch_shapes=scratch,
        compiler_params=pltpu.CompilerParams(
            collective_id=0, has_side_effects=True, vmem_limit_bytes=58 * 2**20
        ),
        name="expert_backward",
    )(out_grad, down_weight[0], held, gates.T, routes.T, copy_pick.T, replica_plan[None, :])
    shapes = (route_grad.shape, hidden_grad.shape, copy_grad.shape)
    kinds = (F32, BF16, BF16)
    route_grad, hidden_grad, copy_grad = pl.pallas_call(
        emit,
        out_shape=tuple(jax.ShapeDtypeStruct(s, k) for s, k in zip(shapes, kinds)),
        in_specs=[here, here, here],
        out_specs=(there, there, there),
        scratch_shapes=[dma((3,))],
        name="results",
    )(*[pltpu.with_memory_space_constraint(a, pltpu.VMEM) for a in (route_grad, hidden_grad, copy_grad)])
    hidden_grad = hidden_grad.reshape(cap, slots, hidden).transpose(1, 0, 2)
    return route_grad.T, hidden_grad[None, None], copy_grad[None]


def solution(mesh):
    groups, slots = mesh.shape["group"], mesh.shape["expert"]
    placed = (
        P(("group", "expert"), None),
        P(("group", "expert"), None),
        P(("group", "expert"), None),
        P(("group", "expert"), None),
        P(),
        P("expert", None, None),
        P("group", "expert", None, None, None),
    )
    return jax.shard_map(
        functools.partial(local, groups, slots),
        mesh=mesh,
        in_specs=placed,
        out_specs=(
            P(("group", "expert"), None),
            P("group", "expert", None, None, None),
            P("expert", "group", None),
        ),
        check_vma=False,
    )
```
